32 devices in a mesh: row: 8 (over z, y), col: 4 (over x, core).
Axes of the slice: x: 2, y: 2, z: 4, core: 2. Of those that a mesh axis runs over, the one named last changes fastest.
Arguments:
- trail_adjoint: float32 [4096, 4096], P('row', 'col'), may hold values from -6 to 6
- lower_new: float32 [4096, 256], P('row', 'col'), may hold values from -0.09375 to 0.09375
- upper_new: float32 [256, 4096], P('row', 'col'), may hold values from -0.09375 to 0.09375
- lower_old_top: float32 [256, 256], replicated, may hold values from -0.375 to 0.375
- lower_old: float32 [4096, 256], P('row', 'col'), may hold values from -0.09375 to 0.09375
- upper_old_left: float32 [256, 256], replicated, may hold values from -0.375 to 0.375
- upper_old: float32 [256, 4096], P('row', 'col'), may hold values from -0.09375 to 0.09375
- diag_lower_new: float32 [256, 256], replicated, as said below
- diag_upper_new: float32 [256, 256], replicated, as said below
- inverse_lower_new: float32 [256, 256], replicated, as said below
- inverse_upper_new: float32 [256, 256], replicated, as said below
- diag_lower_old: float32 [256, 256], replicated, as said below
- diag_upper_old: float32 [256, 256], replicated, as said below
- inverse_lower_old: float32 [256, 256], replicated, as said below
- inverse_upper_old: float32 [256, 256], replicated, as said below
Outputs:
- corner_old: float32 [256, 256], replicated
- strip_top: float32 [256, 256], replicated
- strip_bottom: float32 [4096, 256], P(('row', 'col'))
- band_left: float32 [256, 256], replicated
- band_right: float32 [256, 4096], P(None, 'col')
The draws below stay inside these ranges and needn't reach their ends.
Inputs may be any that keep to these rules, and one draw needn't show every extreme that they name: `diag_lower_new`: unit lower triangular. `diag_upper_new`: upper triangular, diagonal from 1 to 2. `inverse_lower_new`: the inverse of diag_lower_new. `inverse_upper_new`: the inverse of diag_upper_new. `diag_lower_old`: unit lower triangular. `diag_upper_old`: upper triangular, diagonal from 1 to 2. `inverse_lower_old`: the inverse of diag_lower_old. `inverse_upper_old`: the inverse of diag_upper_old.
All inputs are finite; a program needn't handle non-finite values.
Results may differ from the reference program's by a relative error of at most 0.000075.
Values sent between devices are 32-bit elements; how exact they have to be, the bound alone decides.
A program may use at most 128 MiB of HBM per device.

```python
import math
import jax
import jax.numpy as jnp
from jax import lax

B = 256
M = 4096


def triangle_pair(key, marker, downward):
    folded = jax.random.fold_in(key, marker)
    seed_noise, seed_scale = jax.random.split(folded)
    noise = jax.random.normal(seed_noise, (B, B), jnp.float32) * (0.3 / math.sqrt(B))
    identity = jnp.eye(B, dtype=jnp.float32)
    if downward:
        factor = jnp.tril(noise, -1) + identity
    else:
        scales = jax.random.uniform(seed_scale, (B,), jnp.float32, 1.0, 2.0)
        factor = jnp.triu(noise, 1) + jnp.diag(scales)
    inverse = jax.scipy.linalg.solve_triangular(factor, identity, lower=downward)
    return (factor, inverse)


def draw_diag_lower_new(key, part):
    return triangle_pair(key, 1, True)[0]


def draw_inverse_lower_new(key, part):
    return triangle_pair(key, 1, True)[1]


def draw_diag_upper_new(key, part):
    return triangle_pair(key, 2, False)[0]


def draw_inverse_upper_new(key, part):
    return triangle_pair(key, 2, False)[1]


def draw_diag_lower_old(key, part):
    return triangle_pair(key, 3, True)[0]


def draw_inverse_lower_old(key, part):
    return triangle_pair(key, 3, True)[1]


def draw_diag_upper_old(key, part):
    return triangle_pair(key, 4, False)[0]


def draw_inverse_upper_old(key, part):
    return triangle_pair(key, 4, False)[1]


def raised(entries, rng, source, target, parts, factor):
    def block_of(axis_at):
        return (jnp.arange(entries.shape[axis_at]) // (entries.shape[axis_at] // parts)).reshape((-1,) + (1,) * (entries.ndim - 1 - axis_at))

    first = jax.random.permutation(rng, parts)[block_of(target)]
    second = (block_of(target) + parts // 2) % parts
    return jnp.where((block_of(source) == first) | (block_of(source) == second), factor * entries, entries)


def block_levels(stream_key, dims, pieces, low, largest):
    gain = 1.0
    for dim, shards_of in pieces:
        heights = jax.random.uniform(jax.random.fold_in(jax.random.fold_in(stream_key, 6), dim), (shards_of,), jnp.float32, low / len(pieces), largest / len(pieces))
        gain = gain * jnp.repeat(jnp.exp(heights), dims[dim] // shards_of).reshape((-1,) + (1,) * (len(dims) - 1 - dim))
    return gain


def gaussian(own_key, shape, scale, bound, pieces=(), held_as=jnp.bfloat16):
    drawn = scale * jax.random.normal(own_key, shape, jnp.float32)
    if pieces:
        drawn = drawn * block_levels(own_key, shape, pieces, -0.22, 0.18)
    return jnp.clip(drawn, -bound, bound).astype(held_as)


def noise_with(own_key, extent, spread, bound, shards, heavy, kind=jnp.bfloat16):
    drawn = spread * jax.random.normal(own_key, extent, jnp.float32)
    if shards:
        drawn = drawn * block_levels(own_key, extent, shards, -0.22, 0.18)
    return jnp.clip(raised(drawn, jax.random.fold_in(own_key, 3), *heavy), -bound, bound).astype(kind)


def setup_inputs(seed: int = 0) -> dict:
    streams_of = jax.random.split(jax.random.key(seed), 16)
    trail_adjoint = noise_with(streams_of[0], (M, M), 1.0, 6.0, ((0, 8), (1, 4)), (1, 0, 8, 2.0), jnp.float32)
    lower_new = gaussian(streams_of[1], (M, B), M ** -0.5, 0.09375, ((0, 8), (1, 4)), jnp.float32)
    upper_new = gaussian(streams_of[2], (B, M), M ** -0.5, 0.09375, ((0, 8), (1, 4)), jnp.float32)
    lower_old_top = gaussian(streams_of[3], (B, B), B ** -0.5, 0.375, (), jnp.float32)
    lower_old = gaussian(streams_of[4], (M, B), M ** -0.5, 0.09375, ((0, 8), (1, 4)), jnp.float32)
    upper_old_left = gaussian(streams_of[5], (B, B), B ** -0.5, 0.375, (), jnp.float32)
    upper_old = gaussian(streams_of[6], (B, M), M ** -0.5, 0.09375, ((0, 8), (1, 4)), jnp.float32)
    diag_lower_new = draw_diag_lower_new(jax.random.fold_in(streams_of[15], 71), 0)
    diag_upper_new = draw_diag_upper_new(jax.random.fold_in(streams_of[15], 71), 0)
    inverse_lower_new = draw_inverse_lower_new(jax.random.fold_in(streams_of[15], 71), 0)
    inverse_upper_new = draw_inverse_upper_new(jax.random.fold_in(streams_of[15], 71), 0)
    diag_lower_old = draw_diag_lower_old(jax.random.fold_in(streams_of[15], 71), 0)
    diag_upper_old = draw_diag_upper_old(jax.random.fold_in(streams_of[15], 71), 0)
    inverse_lower_old = draw_inverse_lower_old(jax.random.fold_in(streams_of[15], 71), 0)
    inverse_upper_old = draw_inverse_upper_old(jax.random.fold_in(streams_of[15], 71), 0)
    return dict(trail_adjoint=trail_adjoint, lower_new=lower_new, upper_new=upper_new, lower_old_top=lower_old_top, lower_old=lower_old, upper_old_left=upper_old_left, upper_old=upper_old, diag_lower_new=diag_lower_new, diag_upper_new=diag_upper_new, inverse_lower_new=inverse_lower_new, inverse_upper_new=inverse_upper_new, diag_lower_old=diag_lower_old, diag_upper_old=diag_upper_old, inverse_lower_old=inverse_lower_old, inverse_upper_old=inverse_upper_old)


precise = lax.Precision.HIGHEST

def product(left, right):
    return jnp.dot(left, right, precision=precise)

def diag_adjoint(lower_factor, upper_factor, lower_inverse, upper_inverse, lower_grad, upper_grad):
    inner = jnp.tril(product(lower_factor.T, lower_grad), -1) + jnp.triu(product(upper_grad, upper_factor.T))
    return product(product(lower_inverse.T, inner), upper_inverse.T)

def reference(trail_adjoint, lower_new, upper_new, lower_old_top, lower_old, upper_old_left, upper_old, diag_lower_new, diag_upper_new, inverse_lower_new, inverse_upper_new, diag_lower_old, diag_upper_old, inverse_lower_old, inverse_upper_old):
    lower_adj_new = -product(trail_adjoint, upper_new.T)
    upper_adj_new = -product(lower_new.T, trail_adjoint)
    strip_new = product(lower_adj_new, inverse_upper_new.T)
    band_new = product(inverse_lower_new.T, upper_adj_new)
    corner_new = diag_adjoint(diag_lower_new, diag_upper_new, inverse_lower_new, inverse_upper_new, -product(band_new, upper_new.T), -product(lower_new.T, strip_new))
    strip_top = product(-(product(corner_new, upper_old_left.T) + product(band_new, upper_old.T)), inverse_upper_old.T)
    strip_bottom = product(-(product(strip_new, upper_old_left.T) + product(trail_adjoint, upper_old.T)), inverse_upper_old.T)
    band_left = product(inverse_lower_old.T, -(product(lower_old_top.T, corner_new) + product(lower_old.T, strip_new)))
    band_right = product(inverse_lower_old.T, -(product(lower_old_top.T, band_new) + product(lower_old.T, trail_adjoint)))
    lower_grad = -(product(band_left, upper_old_left.T) + product(band_right, upper_old.T))
    upper_grad = -(product(lower_old_top.T, strip_top) + product(lower_old.T, strip_bottom))
    corner_old = diag_adjoint(diag_lower_old, diag_upper_old, inverse_lower_old, inverse_upper_old, lower_grad, upper_grad)
    return (corner_old, strip_top, strip_bottom, band_left, band_right)
```

```python
import functools

import jax
import jax.numpy as jnp
from jax import lax
from jax.experimental import pallas as pl
from jax.experimental.pallas import tpu as pltpu
from jax.sharding import PartitionSpec as P

f32, bf16 = jnp.float32, jnp.bfloat16
LIMIT = 48 << 20
NN, NT = ((1,), (0,)), ((1,), (1,))


def split(x):
    high = x.astype(bf16)
    return high, (x - high.astype(f32)).astype(bf16)


def mul(a, b, dims=NN):
    def one(x, y):
        return lax.dot_general(x, y, (dims, ((), ())), preferred_element_type=f32)

    return one(a[0], b[0]) + (one(a[0], b[1]) + one(a[1], b[0]))


def start(axis, n, me, source, target, send, recv):
    copies = []
    for d in range(1, n):
        peer = lax.rem(me + d, n)
        copy = pltpu.make_async_remote_copy(
            src_ref=source(peer),
            dst_ref=target,
            send_sem=send.at[d],
            recv_sem=recv.at[d],
            device_id={axis: peer},
            device_id_type=pl.DeviceIdType.MESH,
        )
        copy.start()
        copies.append(copy)
    return copies


def arrive(copies):
    for copy in copies:
        copy.wait_recv()


def kernel(
    nr, nc, ny, a_hbm, un_ref, uo_ref, ln_ref, lo_ref, lot_hbm, uol_hbm, iln_hbm, iun_hbm, ilo_hbm, iuo_hbm,
    strip_ref, band_ref, both_ref, left_ref,
    a_ref, ah, al, xu, xl, ut, lt, pb, ps, ry, sz, rz, rp, bc, uni, lni,
    pa, ra, sa, ta, ga, pl_, rl, sl, tl, gl,
    sq, asem, qsem, osem, rs_send, rs_recv, cs_send, cs_recv,
):
    r, c = lax.axis_index("row"), lax.axis_index("col")
    rows, cols = a_hbm.shape
    wu, wl = cols // nr, rows // nc
    width = iln_hbm.shape[0]
    hl = width // nc
    nz = nr // ny
    z, y = r // ny, lax.rem(r, ny)
    far = [nz // 2] * (nz > 1) + [k for k in range(nz - 1, 0, -1) if k != nz // 2]
    load = pltpu.make_async_copy(a_hbm, a_ref, asem)
    squares = (iuo_hbm, uol_hbm, iun_hbm, iln_hbm, lot_hbm, ilo_hbm)
    loads = [pltpu.make_async_copy(m, sq.at[i], qsem.at[i]) for i, m in enumerate(squares)]
    own = [
        pltpu.make_async_copy(un_ref.at[:, pl.ds(pl.multiple_of(r * wu, wu), wu)], xu.at[0, r], osem.at[0]),
        pltpu.make_async_copy(uo_ref.at[:, pl.ds(pl.multiple_of(r * wu, wu), wu)], xu.at[1, r], osem.at[1]),
        pltpu.make_async_copy(ln_ref.at[:, pl.ds(pl.multiple_of(c * wl, wl), wl)], xl.at[0, c], osem.at[2]),
        pltpu.make_async_copy(lo_ref.at[:, pl.ds(pl.multiple_of(c * wl, wl), wl)], xl.at[1, c], osem.at[3]),
    ]
    for copy in own + loads:
        copy.start()
    load.start()
    barrier = pltpu.get_barrier_semaphore()
    for d in range(1, nr):
        pl.semaphore_signal(barrier, inc=1, device_id={"row": lax.rem(r + d, nr)}, device_id_type=pl.DeviceIdType.MESH)
    for d in range(1, nc):
        pl.semaphore_signal(barrier, inc=1, device_id={"col": lax.rem(c + d, nc)}, device_id_type=pl.DeviceIdType.MESH)
    pl.semaphore_wait(barrier, nr + nc - 2)

    def ucol(i):
        return pl.ds(pl.multiple_of(i * wu, wu), wu)

    def lcol(i):
        return pl.ds(pl.multiple_of(i * wl, wl), wl)

    sent = []

    def row_stage(k, source, target):
        copies = start("row", nr, r, source, target, rs_send.at[k], rs_recv.at[k])
        sent.extend(copies)
        return copies

    def col_stage(k, source, target):
        copies = start("col", nc, c, source, target, cs_send.at[k], cs_recv.at[k])
        sent.extend(copies)
        return copies

    def push(stage, index, source, target, zi, yi):
        copy = pltpu.make_async_remote_copy(
            src_ref=source,
            dst_ref=target,
            send_sem=rs_send.at[stage, index],
            recv_sem=rs_recv.at[stage, index],
            device_id={"row": zi * ny + yi},
            device_id_type=pl.DeviceIdType.MESH,
        )
        copy.start()
        sent.append(copy)
        return copy

    def across(stage, k, source, slot):
        return [push(stage, k * ny + d, source, slot, z, lax.rem(y + d, ny)) for d in range(1, ny)]

    def gather_start(stage, source, slot):
        along = {k: push(stage, k, source, slot(r), lax.rem(z + k, nz), y) for k in far}
        return along, across(stage + 1, 0, source, slot(r))

    def gather_pass(stage, state, slot):
        along, over = state
        for k in far[::-1]:
            along[k].wait_recv()
            here = slot(lax.rem(z - k + nz, nz) * ny + y)
            over.extend(across(stage + 1, k, here, here))
        return over

    cores = 2 if nc % 2 == 0 else 1
    nx = nc // cores
    x, core = c // cores, lax.rem(c, cores)

    def toss(stage, index, source, target, peer):
        copy = pltpu.make_async_remote_copy(
            src_ref=source,
            dst_ref=target,
            send_sem=cs_send.at[stage, index],
            recv_sem=cs_recv.at[stage, index],
            device_id={"col": peer},
            device_id_type=pl.DeviceIdType.MESH,
        )
        copy.start()
        sent.append(copy)
        return copy

    def twin(stage, k, source, target):
        if cores == 1:
            return []
        return [toss(stage, nx + k, source, target, x * cores + 1 - core)]

    def spread_start(stage, source, slot):
        along = [toss(stage, k, source, slot(c), lax.rem(x + k, nx) * cores + core) for k in range(1, nx)]
        return along, twin(stage, 0, source, slot(c))

    def spread_end(stage, state, slot):
        along, near = state
        for k in range(1, nx):
            along[k - 1].wait_recv()
            here = slot(lax.rem(x - k + nx, nx) * cores + core)
            near = near + twin(stage, k, here, here)
        return near

    u0 = row_stage(0, lambda p: un_ref.at[:, ucol(p)], xu.at[0, r])
    u0 = u0 + row_stage(11, lambda p: uo_ref.at[:, ucol(p)], xu.at[1, r])
    l0 = col_stage(0, lambda p: ln_ref.at[:, lcol(p)], xl.at[0, c])
    l0 = l0 + col_stage(7, lambda p: lo_ref.at[:, lcol(p)], xl.at[1, c])
    for copy in own + loads:
        copy.wait()
    iuo, iun = split(sq[0]), split(sq[2])
    mix_u = split(mul(split(mul(iuo, split(sq[1]))), iun))
    ilo = sq[5]
    mix_l = mul(split(mul(split(sq[3]), split(sq[4]))), split(ilo))
    mix_l, ilo, iln = split(mix_l.T), split(ilo.T), split(sq[3].T)
    uslot = lambda i: ut.at[:, ucol(i)]
    lslot = lambda i: lt.at[:, lcol(i)]
    arrive(l0)
    ln = split(xl[0].reshape(width, wl))
    lt[:, lcol(c)] = mul(ilo, split(xl[1].reshape(width, wl))) - mul(mix_l, ln)
    l1 = spread_start(1, lslot(c), lslot)
    arrive(u0)
    un = split(xu[0].reshape(width, wu))
    ut[:, ucol(r)] = mul(iuo, split(xu[1].reshape(width, wu))) - mul(mix_u, un)
    along, over = gather_start(1, uslot(r), uslot)
    uni[...] = mul(iun, un)
    lni[...] = mul(iln, ln)
    load.wait()
    high, low = split(a_ref[...])
    ah[...] = high
    al[...] = low
    arrive(spread_end(1, l1, lslot))
    lts = split(lt[...])
    b0 = {}
    later = far[::-1]
    for k in far + [0]:
        zt = lax.rem(z + k, nz)
        here = pl.ds(pl.multiple_of(zt * ny * wu, ny * wu), ny * wu)
        pb[:, here] = -mul(lts, (ah[:, here], al[:, here]))
        b0[k] = [
            push(3, k * ny + d, pb.at[:, ucol(zt * ny + lax.rem(y + d, ny))], ry.at[k, d], z, lax.rem(y + d, ny))
            for d in range(1, ny)
        ]
        if later:
            m = later.pop(0)
            along[m].wait_recv()
            at = uslot(lax.rem(z - m + nz, nz) * ny + y)
            over.extend(across(2, m, at, at))
    b1 = {}
    for k in far + [0]:
        arrive(b0[k])
        zt = lax.rem(z + k, nz)
        total = pb[:, ucol(zt * ny + y)]
        for d in range(1, ny):
            total = total + ry[k, d]
        if k:
            sz[k] = total
            b1[k] = push(4, k, sz.at[k], rz.at[k], zt, y)
        else:
            rz[0] = total
    arrive(over)
    uts = split(ut[...])
    tile = 2 * wl
    for i in range(rows // tile):
        here = slice(i * tile, (i + 1) * tile)
        ps[here] = -mul((ah[here], al[here]), uts, NT)
    p0 = col_stage(2, lambda p: ps.at[lcol(p)], rp.at[c])
    rp[c] = ps[lcol(c)]

    def small_cols(stage, part, got):
        high = part.shape[0] // nc
        at = lambda p: part.at[pl.ds(pl.multiple_of(p * high, high), high)]
        copies = col_stage(stage, at, got.at[c])
        got[c] = part[pl.ds(pl.multiple_of(c * high, high), high)]
        return copies

    def small_rows(stage, copies, got, send, take):
        arrive(copies)
        total = got[0]
        for i in range(1, nc):
            total = total + got[i]
        each = send.shape[1]
        for i in range(nr):
            send[i] = total[i * each : (i + 1) * each]
        copies = row_stage(stage, lambda p: send.at[p], take.at[r])
        take[r] = send[r]
        return copies

    def back_rows(stage, copies, take, whole):
        arrive(copies)
        total = take[0]
        for i in range(1, nr):
            total = total + take[i]
        whole[r] = total
        return row_stage(stage, lambda p: whole.at[r], whole.at[r])

    def back_cols(stage, copies, whole, out):
        arrive(copies)
        copies = spread_start(stage, whole, lambda i: out.at[i])
        out[c] = whole[...]
        return copies

    arrive([b1[k] for k in far])
    band = rz[0]
    for k in range(1, nz):
        band = band + rz[k]
    bc[...] = band
    bslot = lambda i: band_ref.at[:, ucol(i)]
    b2 = gather_start(5, bc, bslot)
    band_ref[:, ucol(r)] = band
    pl_[...] = -mul(split(band), split(uni[...]), NT)
    left = small_cols(3, pl_, rl)
    arrive(p0)
    strip = rp[0]
    for i in range(1, nc):
        strip = strip + rp[i]
    strip_ref[...] = strip
    strip = split(strip)
    pa[:width] = -mul(split(lni[...]), strip)
    pa[width:] = -mul(split(lt[:, lcol(c)]), strip)
    both = small_cols(4, pa, ra)
    left = small_rows(7, left, rl, sl, tl)
    both = small_rows(8, both, ra, sa, ta)
    over = gather_pass(5, b2, bslot)
    left = back_rows(9, left, tl, gl)
    both = back_rows(10, both, ta, ga)
    left = back_cols(5, left, gl, left_ref)
    both = back_cols(6, both, ga, both_ref)
    left = spread_end(5, left, lambda i: left_ref.at[i])
    both = spread_end(6, both, lambda i: both_ref.at[i])
    arrive(left)
    arrive(both)
    arrive(over)
    for copy in sent:
        copy.wait_send()


def finish(strip_ref, band_ref, both_ref, left_ref, corner, top, bottom, left, right, sem):
    width = left_ref.shape[0]
    pairs = (
        (band_ref, right), (strip_ref, bottom), (left_ref, left),
        (both_ref.at[pl.ds(width, width)], corner), (both_ref.at[pl.ds(0, width)], top),
    )
    copies = [pltpu.make_async_copy(source, target, sem.at[i]) for i, (source, target) in enumerate(pairs)]
    for copy in copies:
        copy.start()
    for copy in copies:
        copy.wait()


def body(an, ln, un, lot, lo, uol, uo, dln, dun, iln, iun, dlo, duo, ilo, iuo):
    nr, nc = lax.axis_size("row"), lax.axis_size("col")
    rows, cols = an.shape
    width = iln.shape[0]
    wu, wl = cols // nr, rows // nc
    ny = nc // 2 if nc % 2 == 0 and nr % max(nc // 2, 1) == 0 else 1
    nz = nr // ny
    vm = pl.BlockSpec(memory_space=pltpu.VMEM)
    hbm = pl.BlockSpec(memory_space=pltpu.HBM)
    V = pltpu.VMEM

    def chain(size):
        high = size // nc
        whole = V((nr, high // nr, width), f32)
        return [V((size, width), f32), V((nc, high, width), f32), whole, whole, whole]

    D = pltpu.SemaphoreType.DMA
    operands = (an, un, uo, ln.T, lo.T, lot, uol, iln, iun, ilo, iuo)
    results = pl.pallas_call(
        functools.partial(kernel, nr, nc, ny),
        out_shape=(
            V((wl, width), f32),
            V((width, cols), f32),
            V((nc, nr, 2 * width // nc // nr, width), f32),
            V((nc, nr, width // nc // nr, width), f32),
        ),
        in_specs=[hbm] * 11,
        out_specs=(vm, vm, vm, vm),
        scratch_shapes=[
            V((rows, cols), f32), V((rows, cols), bf16), V((rows, cols), bf16),
            V((2, nr, width // nr, wu), f32), V((2, nc, width // nc, wl), f32),
            V((width, cols), f32), V((width, rows), f32),
            V((width, cols), f32), V((rows, width), f32),
            V((nz, ny, width, wu), f32), V((nz, width, wu), f32), V((nz, width, wu), f32),
            V((nc, wl, width), f32), V((width, wu), f32),
            V((width, wu), f32), V((width, wl), f32),
            *chain(2 * width), *chain(width),
            V((6, width, width), f32), D, D((6,)), D((4,)), D((12, nr)), D((12, nr)), D((8, nc)), D((8, nc)),
        ],
        compiler_params=pltpu.CompilerParams(collective_id=0, has_side_effects=True, vmem_limit_bytes=LIMIT),
    )(*[pltpu.with_memory_space_constraint(v, pltpu.HBM) for v in operands])
    strip, band, both, left = results
    shapes = [(width, width), (width, width), strip.shape, (width, width), band.shape]
    return pl.pallas_call(
        finish,
        out_shape=[jax.ShapeDtypeStruct(shape, f32) for shape in shapes],
        in_specs=[vm] * 4,
        out_specs=[hbm] * 5,
        scratch_shapes=[D((5,))],
        compiler_params=pltpu.CompilerParams(vmem_limit_bytes=1 << 20),
    )(strip, band, both.reshape(2 * width, width), left.reshape(width, width))


def solution(mesh):
    two, whole = P("row", "col"), P()
    return jax.shard_map(
        body,
        mesh=mesh,
        in_specs=(two, two, two, whole, two, whole, two) + (whole,) * 8,
        out_specs=(P(), P(), P(("row", "col"), None), P(), P(None, "col")),
        check_vma=False,
    )
```

```python
import functools

import jax
import jax.numpy as jnp
from jax import lax
from jax.experimental import pallas as pl
from jax.experimental.pallas import tpu as pltpu
from jax.sharding import PartitionSpec as P

f32, bf16 = jnp.float32, jnp.bfloat16
NN, NT = ((1,), (0,)), ((1,), (1,))
LIMIT = 48 << 20


def split(x):
    high = x.astype(bf16)
    return high, (x - high.astype(f32)).astype(bf16)


def mul(a, b, dims=NN):
    def one(x, y):
        return lax.dot_general(x, y, (dims, ((), ())), preferred_element_type=f32)

    return one(a[0], b[0]) + (one(a[0], b[1]) + one(a[1], b[0]))


def flip(z, k):
    bit = 1
    while bit <= k:
        if k & bit:
            z = z + bit - 2 * bit * lax.rem(z // bit, 2)
        bit *= 2
    return z


def arrive(copies):
    for copy in copies:
        copy.wait_recv()


def kernel(
    nr, nc, ny, a_hbm, un_hbm, uo_hbm, ln_hbm, lo_hbm, lot_hbm, uol_hbm, iln_hbm, iun_hbm, ilo_hbm, iuo_hbm,
    strip_ref, band_ref, both_ref, top_ref,
    a_ref, ah, al, xu, xl, vh, vl, pb, ps, ry, sz, rz, rp, bc, gp, gr, gc,
    pt, rt, st, tt, gt, sq,
    asem, qsem, osem, rs_send, rs_recv, cs_send, cs_recv,
):
    r, c = lax.axis_index("row"), lax.axis_index("col")
    rows, cols = a_hbm.shape
    wl = rows // nc
    width = iln_hbm.shape[0]
    hu = width // nr
    nz = nr // ny
    z, y = r // ny, lax.rem(r, ny)
    even = nz & (nz - 1) == 0
    hops = list(range(1, nz))
    reach = lambda k: flip(z, k) if even else lax.rem(z + k, nz)
    origin = lambda k: flip(z, k) if even else lax.rem(z - k + nz, nz)
    cores = 2 if nc % 2 == 0 else 1
    nx = nc // cores
    x, core = c // cores, lax.rem(c, cores)

    load = pltpu.make_async_copy(a_hbm, a_ref, asem)
    squares = (iuo_hbm, uol_hbm, iun_hbm, iln_hbm, lot_hbm, ilo_hbm)
    loads = [pltpu.make_async_copy(m, sq.at[i], qsem.at[i]) for i, m in enumerate(squares)]
    own = [
        pltpu.make_async_copy(source, target, osem.at[i])
        for i, (source, target) in enumerate(
            [(un_hbm, xu.at[0, r]), (uo_hbm, xu.at[1, r]), (ln_hbm, xl.at[0, c]), (lo_hbm, xl.at[1, c])]
        )
    ]
    for copy in loads + own:
        copy.start()
    load.start()
    barrier = pltpu.get_barrier_semaphore()
    for d in range(1, nr):
        pl.semaphore_signal(barrier, inc=1, device_id={"row": lax.rem(r + d, nr)}, device_id_type=pl.DeviceIdType.MESH)
    for d in range(1, nc):
        pl.semaphore_signal(barrier, inc=1, device_id={"col": lax.rem(c + d, nc)}, device_id_type=pl.DeviceIdType.MESH)
    pl.semaphore_wait(barrier, nr + nc - 2)

    def lrow(i):
        return pl.ds(pl.multiple_of(i * wl, wl), wl)

    def urow(i):
        return pl.ds(pl.multiple_of(i * hu, hu), hu)

    sent = []

    def put(axis, peer, source, target, send, recv):
        copy = pltpu.make_async_remote_copy(
            src_ref=source,
            dst_ref=target,
            send_sem=send,
            recv_sem=recv,
            device_id={axis: peer},
            device_id_type=pl.DeviceIdType.MESH,
        )
        copy.start()
        sent.append(copy)
        return copy

    def push(stage, index, source, target, peer):
        return put("row", peer, source, target, rs_send.at[stage, index], rs_recv.at[stage, index])

    def toss(stage, index, source, target, peer):
        return put("col", peer, source, target, cs_send.at[stage, index], cs_recv.at[stage, index])

    def across(stage, k, source, slot):
        return [push(stage, k * ny + d, source, slot, z * ny + lax.rem(y + d, ny)) for d in range(1, ny)]

    def gather_start(stage, source, slot):
        over = across(stage + 1, 0, source, slot(r))
        along = {k: push(stage, k, source, slot(r), reach(k) * ny + y) for k in hops}
        return along, over

    def gather_pass(stage, state, slot, k):
        along, over = state
        along[k].wait_recv()
        here = slot(origin(k) * ny + y)
        over.extend(across(stage + 1, k, here, here))

    def twin(stage, k, source, target):
        if cores == 1:
            return []
        return [toss(stage, nx + k, source, target, x * cores + 1 - core)]

    def spread_start(stage, source, slot):
        along = [toss(stage, k, source, slot(c), lax.rem(x + k, nx) * cores + core) for k in range(1, nx)]
        return along, twin(stage, 0, source, slot(c))

    def spread_end(stage, state, slot):
        along, near = state
        for k in range(1, nx):
            along[k - 1].wait_recv()
            here = slot(lax.rem(x - k + nx, nx) * cores + core)
            near = near + twin(stage, k, here, here)
        return near

    def row_stage(stage, source, target):
        peers = [lax.rem(r + d, nr) for d in range(1, nr)]
        return [push(stage, d, source(p), target, p) for d, p in enumerate(peers, 1)]

    def col_stage(stage, source, target):
        peers = [lax.rem(c + d, nc) for d in range(1, nc)]
        return [toss(stage, d, source(p), target, p) for d, p in enumerate(peers, 1)]

    lslot = [lambda i: xl.at[0, i], lambda i: xl.at[1, i]]
    uslot = [lambda i: xu.at[0, i], lambda i: xu.at[1, i]]
    low = [spread_start(0, ln_hbm, lslot[0]), spread_start(1, lo_hbm, lslot[1])]
    up = [gather_start(0, un_hbm, uslot[0]), gather_start(2, uo_hbm, uslot[1])]
    for copy in own + loads:
        copy.wait()
    iuo, iun = split(sq[0]), split(sq[2])
    mix_u = split(mul(split(mul(iuo, split(sq[1]))), iun))
    ilo = sq[5]
    mix_l = mul(split(mul(split(sq[3]), split(sq[4]))), split(ilo))
    mix_l, ilo, iln = split(mix_l.T), split(ilo.T), split(sq[3].T)
    load.wait()
    high, rest = split(a_ref[...])
    ah[...] = high
    al[...] = rest
    gather_pass(0, up[0], uslot[0], hops[0])
    near = spread_end(0, low[0], lslot[0])
    near = near + spread_end(1, low[1], lslot[1])
    arrive(near)
    ln, lo = split(xl[0].reshape(width, rows)), split(xl[1].reshape(width, rows))
    lts = split(mul(ilo, lo) - mul(mix_l, ln))
    lns = split(mul(iln, ln))
    for i in range(cols // width):
        here = slice(i * width, (i + 1) * width)
        pb[:, here] = -mul(lts, (ah[:, here], al[:, here]))
    b0 = {}
    for k in hops[::-1] + [0]:
        zt = reach(k) if k else z
        peers = [zt * ny + lax.rem(y + d, ny) for d in range(1, ny)]
        b0[k] = [
            push(4, k * ny + d, pb.at[urow(p)], ry.at[k, d], z * ny + lax.rem(y + d, ny)) for d, p in enumerate(peers, 1)
        ]
    for k in hops[1:]:
        gather_pass(0, up[0], uslot[0], k)
    gather_pass(2, up[1], uslot[1], hops[0])
    b1 = {}
    for k in hops[::-1] + [0]:
        arrive(b0[k])
        zt = reach(k) if k else z
        total = pb[urow(zt * ny + y)]
        for d in range(1, ny):
            total = total + ry[k, d]
        if k:
            sz[k] = total
            b1[k] = push(5, k, sz.at[k], rz.at[k], zt * ny + y)
        else:
            rz[0] = total
    for k in hops[1:]:
        gather_pass(2, up[1], uslot[1], k)
    for state in up:
        arrive(state[1])
    for i in range(cols // width):
        here = slice(i * width, (i + 1) * width)
        un, uo = split(xu[0, :, :, here].reshape(width, width)), split(xu[1, :, :, here].reshape(width, width))
        vh[:width, here], vl[:width, here] = split(mul(iuo, uo) - mul(mix_u, un))
        vh[width:, here], vl[width:, here] = split(mul(iun, un))
    for i in range(rows // width):
        here = slice(i * width, (i + 1) * width)
        ps[here] = -mul((ah[here], al[here]), (vh[:width], vl[:width]), NT)
    pt[...] = -mul(lns, split(ps[...]))
    each = width // nc
    part = lambda p: pt.at[pl.ds(pl.multiple_of(p * each, each), each)]
    t0 = col_stage(3, part, rt.at[c])
    rt[c] = part(c)[...]
    p0 = col_stage(2, lambda p: ps.at[lrow(p)], rp.at[c])
    rp[c] = ps[lrow(c)]
    arrive([b1[k] for k in hops])
    band = rz[0]
    for k in hops:
        band = band + rz[k]
    bc[...] = band
    bslot = lambda i: band_ref.at[urow(i)]
    b2 = gather_start(6, bc, bslot)
    band_ref[urow(r)] = band
    gp[...] = -mul(split(band), (vh[...], vl[...]), NT)
    g0 = col_stage(4, lambda p: gp, gr.at[c])
    gr[c] = gp[...]
    arrive(t0)
    total = rt[0]
    for i in range(1, nc):
        total = total + rt[i]
    few = each // nr
    for i in range(nr):
        st[i] = total[i * few : (i + 1) * few]
    t1 = row_stage(10, lambda p: st.at[p], tt.at[r])
    tt[r] = st[r]
    gather_pass(6, b2, bslot, hops[0])
    arrive(g0)
    total = gr[0]
    for i in range(1, nc):
        total = total + gr[i]
    gc[...] = total
    cslot = lambda i: both_ref.at[urow(i)]
    g1 = gather_start(8, gc, cslot)
    both_ref[urow(r)] = total
    arrive(t1)
    total = tt[0]
    for i in range(1, nr):
        total = total + tt[i]
    gt[r] = total
    t2 = row_stage(11, lambda p: gt.at[r], gt.at[r])
    for k in hops[1:]:
        gather_pass(6, b2, bslot, k)
    arrive(p0)
    strip = rp[0]
    for i in range(1, nc):
        strip = strip + rp[i]
    strip_ref[...] = strip
    arrive(t2)
    tslot = lambda i: top_ref.at[i]
    t3 = spread_start(5, gt, tslot)
    top_ref[c] = gt[...]
    for k in hops:
        gather_pass(8, g1, cslot, k)
    arrive(spread_end(5, t3, tslot))
    arrive(b2[1])
    arrive(g1[1])
    for copy in sent:
        copy.wait_send()


def finish(strip_ref, band_ref, both_ref, top_ref, corner, top, bottom, left, right, sem):
    width = top_ref.shape[0]
    pairs = (
        (band_ref, right), (strip_ref, bottom), (top_ref, top),
        (both_ref.at[:, pl.ds(0, width)], corner), (both_ref.at[:, pl.ds(width, width)], left),
    )
    copies = [pltpu.make_async_copy(source, target, sem.at[i]) for i, (source, target) in enumerate(pairs)]
    for copy in copies:
        copy.start()
    for copy in copies:
        copy.wait()


def body(an, ln, un, lot, lo, uol, uo, dln, dun, iln, iun, dlo, duo, ilo, iuo):
    nr, nc = lax.axis_size("row"), lax.axis_size("col")
    rows, cols = an.shape
    width = iln.shape[0]
    hu, wl, each = width // nr, rows // nc, width // nc
    ny = nc // 2 if nc % 2 == 0 and nr % max(nc // 2, 1) == 0 else 1
    nz = nr // ny
    vm = pl.BlockSpec(memory_space=pltpu.VMEM)
    hbm = pl.BlockSpec(memory_space=pltpu.HBM)
    V, D = pltpu.VMEM, pltpu.SemaphoreType.DMA
    whole = V((nr, each // nr, width), f32)
    operands = (an, un, uo, ln.T, lo.T, lot, uol, iln, iun, ilo, iuo)
    strip, band, both, top = pl.pallas_call(
        functools.partial(kernel, nr, nc, ny),
        out_shape=(
            V((wl, width), f32), V((width, cols), f32), V((width, 2 * width), f32), V((nc, nr, each // nr, width), f32)
        ),
        in_specs=[hbm] * 11,
        out_specs=(vm, vm, vm, vm),
        scratch_shapes=[
            V((rows, cols), f32), V((rows, cols), bf16), V((rows, cols), bf16),
            V((2, nr, hu, cols), f32), V((2, nc, each, rows), f32),
            V((2 * width, cols), bf16), V((2 * width, cols), bf16),
            V((width, cols), f32), V((rows, width), f32),
            V((nz, ny, hu, cols), f32), V((nz, hu, cols), f32), V((nz, hu, cols), f32),
            V((nc, wl, width), f32), V((hu, cols), f32),
            V((hu, 2 * width), f32), V((nc, hu, 2 * width), f32), V((hu, 2 * width), f32),
            V((width, width), f32), V((nc, each, width), f32), whole, whole, whole,
            V((6, width, width), f32),
            D, D((6,)), D((4,)), D((12, nr)), D((12, nr)), D((6, nc)), D((6, nc)),
        ],
        compiler_params=pltpu.CompilerParams(collective_id=0, has_side_effects=True, vmem_limit_bytes=LIMIT),
    )(*[pltpu.with_memory_space_constraint(v, pltpu.HBM) for v in operands])
    shapes = [(width, width), (width, width), strip.shape, (width, width), band.shape]
    return pl.pallas_call(
        finish,
        out_shape=[jax.ShapeDtypeStruct(shape, f32) for shape in shapes],
        in_specs=[vm] * 4,
        out_specs=[hbm] * 5,
        scratch_shapes=[D((5,))],
        compiler_params=pltpu.CompilerParams(vmem_limit_bytes=1 << 20),
    )(strip, band, both, top.reshape(width, width))


def solution(mesh):
    two, whole = P("row", "col"), P()
    return jax.shard_map(
        body,
        mesh=mesh,
        in_specs=(two, two, two, whole, two, whole, two) + (whole,) * 8,
        out_specs=(P(), P(), P(("row", "col"), None), P(), P(None, "col")),
        check_vma=False,
    )
```

```python
import functools

import jax
import jax.numpy as jnp
from jax import lax
from jax.experimental import pallas as pl
from jax.experimental.pallas import tpu as pltpu
from jax.sharding import PartitionSpec as P

f32, bf16 = jnp.float32, jnp.bfloat16
NN, NT = ((1,), (0,)), ((1,), (1,))
LIMIT = 48 << 20


def split(x):
    high = x.astype(bf16)
    return high, (x - high.astype(f32)).astype(bf16)


def mul(a, b, dims=NN):
    def one(x, y):
        return lax.dot_general(x, y, (dims, ((), ())), preferred_element_type=f32)

    return one(a[0], b[0]) + (one(a[0], b[1]) + one(a[1], b[0]))


def flip(z, k):
    bit = 1
    while bit <= k:
        if k & bit:
            z = z + bit - 2 * bit * lax.rem(z // bit, 2)
        bit *= 2
    return z


def arrive(copies):
    for copy in copies:
        copy.wait_recv()


def kernel(
    nr, nc, ny, a_hbm, un_hbm, uo_hbm, ln_hbm, lo_hbm, lot_hbm, uol_hbm, iln_hbm, iun_hbm, ilo_hbm, iuo_hbm,
    strip_ref, band_ref, both_ref, top_ref,
    a_ref, ah, al, xu, xl, vh, vl, pb, ps, ry, sz, rz, rp, bc, gp, gr, gc,
    pt, rt, st, tt, gt, sq,
    asem, qsem, osem, rs_send, rs_recv, cs_send, cs_recv,
):
    r, c = lax.axis_index("row"), lax.axis_index("col")
    rows, cols = a_hbm.shape
    wl = rows // nc
    width = iln_hbm.shape[0]
    hu = width // nr
    nz = nr // ny
    z, y = r // ny, lax.rem(r, ny)
    even = nz & (nz - 1) == 0
    hops = list(range(1, nz))
    reach = lambda k: flip(z, k) if even else lax.rem(z + k, nz)
    origin = lambda k: flip(z, k) if even else lax.rem(z - k + nz, nz)
    cores = 2 if nc % 2 == 0 else 1
    nx = nc // cores
    x, core = c // cores, lax.rem(c, cores)

    load = pltpu.make_async_copy(a_hbm, a_ref, asem)
    squares = (iuo_hbm, uol_hbm, iun_hbm, iln_hbm, lot_hbm, ilo_hbm)
    loads = [pltpu.make_async_copy(m, sq.at[i], qsem.at[i]) for i, m in enumerate(squares)]
    own = [
        pltpu.make_async_copy(source, target, osem.at[i])
        for i, (source, target) in enumerate(
            [(un_hbm, xu.at[0, r]), (uo_hbm, xu.at[1, r]), (ln_hbm, xl.at[0, c]), (lo_hbm, xl.at[1, c])]
        )
    ]
    for copy in loads + own:
        copy.start()
    load.start()
    barrier = pltpu.get_barrier_semaphore()
    for d in range(1, nr):
        pl.semaphore_signal(barrier, inc=1, device_id={"row": lax.rem(r + d, nr)}, device_id_type=pl.DeviceIdType.MESH)
    for d in range(1, nc):
        pl.semaphore_signal(barrier, inc=1, device_id={"col": lax.rem(c + d, nc)}, device_id_type=pl.DeviceIdType.MESH)
    pl.semaphore_wait(barrier, nr + nc - 2)

    def lrow(i):
        return pl.ds(pl.multiple_of(i * wl, wl), wl)

    def urow(i):
        return pl.ds(pl.multiple_of(i * hu, hu), hu)

    sent = []

    def put(axis, peer, source, target, send, recv):
        copy = pltpu.make_async_remote_copy(
            src_ref=source,
            dst_ref=target,
            send_sem=send,
            recv_sem=recv,
            device_id={axis: peer},
            device_id_type=pl.DeviceIdType.MESH,
        )
        copy.start()
        sent.append(copy)
        return copy

    def push(stage, index, source, target, peer):
        return put("row", peer, source, target, rs_send.at[stage, index], rs_recv.at[stage, index])

    def toss(stage, index, source, target, peer):
        return put("col", peer, source, target, cs_send.at[stage, index], cs_recv.at[stage, index])

    quad = nz == 4

    def across(stage, k, zk, slot, source=None):
        here = slot(zk * ny + y)
        base = 3 + 2 * ny + k * ny
        source = here if source is None else source
        return [push(stage, base + d, source, here, z * ny + lax.rem(y + d, ny)) for d in range(1, ny)]

    def gather(stage, source, slot, flat):
        here = slot(r)
        near = lambda i, chunk, origin=None: push(
            stage, i, slot(chunk) if origin is None else origin, slot(chunk), flip(z, 1) * ny + y
        )
        over = across(stage, 0, z, slot, source)
        if not quad:
            along = [push(stage, k, source, here, reach(k) * ny + y) for k in hops]

            def relay(k):
                def step():
                    along[k - 1].wait_recv()
                    over.extend(across(stage, k, origin(k), slot))

                return step

            steps = [relay(k) for k in hops]
            return steps + [lambda: None] * (3 - len(steps)) + [lambda: arrive(over)]
        far = push(stage, 1, source, here, flip(z, 2) * ny + y)
        first = near(0, r, source)
        ends, mid = [], []

        def one():
            if flat:
                arrive(over)
                for d in range(1, ny):
                    ends.append(near(2 + d, z * ny + lax.rem(y - d + ny, ny)))
            else:
                first.wait_recv()
                over.extend(across(stage, 1, flip(z, 1), slot))

        def two():
            far.wait_recv()
            mid.append(near(2, flip(z, 2) * ny + y))
            (ends if flat else over).extend(across(stage, 2, flip(z, 2), slot))

        def three():
            if flat:
                arrive(ends[ny - 1 :])
                for d in range(1, ny):
                    mid.append(near(2 + ny + d, flip(z, 2) * ny + lax.rem(y - d + ny, ny)))
            else:
                arrive(mid)
                over.extend(across(stage, 3, flip(z, 3), slot))

        def four():
            arrive([first] + ends[: ny - 1] + mid if flat else over)

        return [one, two, three, four]

    def twin(stage, k, source, target):
        if cores == 1:
            return []
        return [toss(stage, nx + k, source, target, x * cores + 1 - core)]

    def spread_start(stage, source, slot):
        along = [toss(stage, k, source, slot(c), lax.rem(x + k, nx) * cores + core) for k in range(1, nx)]
        return along, twin(stage, 0, source, slot(c))

    def spread_end(stage, state, slot):
        along, near = state
        for k in range(1, nx):
            along[k - 1].wait_recv()
            here = slot(lax.rem(x - k + nx, nx) * cores + core)
            near = near + twin(stage, k, here, here)
        return near

    def row_stage(stage, source, target):
        peers = [lax.rem(r + d, nr) for d in range(1, nr)]
        return [push(stage, d, source(p), target, p) for d, p in enumerate(peers, 1)]

    def col_stage(stage, source, target):
        peers = [lax.rem(c + d, nc) for d in range(1, nc)]
        return [toss(stage, d, source(p), target, p) for d, p in enumerate(peers, 1)]

    lslot = [lambda i: xl.at[0, i], lambda i: xl.at[1, i]]
    uslot = [lambda i: xu.at[0, i], lambda i: xu.at[1, i]]
    low = [spread_start(0, ln_hbm, lslot[0]), spread_start(1, lo_hbm, lslot[1])]
    up = [gather(0, un_hbm, uslot[0], False), gather(1, uo_hbm, uslot[1], True)]
    for copy in own + loads:
        copy.wait()
    iuo, iun = split(sq[0]), split(sq[2])
    mix_u = split(mul(split(mul(iuo, split(sq[1]))), iun))
    ilo = sq[5]
    mix_l = mul(split(mul(split(sq[3]), split(sq[4]))), split(ilo))
    mix_l, ilo, iln = split(mix_l.T), split(ilo.T), split(sq[3].T)
    load.wait()
    high, rest = split(a_ref[...])
    ah[...] = high
    al[...] = rest
    up[0][0]()
    up[1][0]()
    up[0][1]()
    near = spread_end(0, low[0], lslot[0])
    near = near + spread_end(1, low[1], lslot[1])
    arrive(near)
    ln, lo = split(xl[0].reshape(width, rows)), split(xl[1].reshape(width, rows))
    lts = split(mul(ilo, lo) - mul(mix_l, ln))
    lns = split(mul(iln, ln))
    for i in range(cols // width):
        here = slice(i * width, (i + 1) * width)
        pb[:, here] = -mul(lts, (ah[:, here], al[:, here]))
    b0 = {}
    for k in hops[::-1] + [0]:
        zt = reach(k) if k else z
        peers = [zt * ny + lax.rem(y + d, ny) for d in range(1, ny)]
        b0[k] = [
            push(4, k * ny + d, pb.at[urow(p)], ry.at[k, d], z * ny + lax.rem(y + d, ny)) for d, p in enumerate(peers, 1)
        ]
    up[1][1]()
    up[0][2]()
    b1 = {}
    for k in hops[::-1] + [0]:
        arrive(b0[k])
        zt = reach(k) if k else z
        total = pb[urow(zt * ny + y)]
        for d in range(1, ny):
            total = total + ry[k, d]
        if k:
            sz[k] = total
            b1[k] = push(5, k, sz.at[k], rz.at[k], zt * ny + y)
        else:
            rz[0] = total
    up[1][2]()
    up[0][3]()
    up[1][3]()
    for i in range(cols // width):
        here = slice(i * width, (i + 1) * width)
        un, uo = split(xu[0, :, :, here].reshape(width, width)), split(xu[1, :, :, here].reshape(width, width))
        vh[:width, here], vl[:width, here] = split(mul(iuo, uo) - mul(mix_u, un))
        vh[width:, here], vl[width:, here] = split(mul(iun, un))
    for i in range(rows // width):
        here = slice(i * width, (i + 1) * width)
        ps[here] = -mul((ah[here], al[here]), (vh[:width], vl[:width]), NT)
    pt[...] = -mul(lns, split(ps[...]))
    each = width // nc
    part = lambda p: pt.at[pl.ds(pl.multiple_of(p * each, each), each)]
    t0 = col_stage(3, part, rt.at[c])
    rt[c] = part(c)[...]
    p0 = col_stage(2, lambda p: ps.at[lrow(p)], rp.at[c])
    rp[c] = ps[lrow(c)]
    arrive([b1[k] for k in hops])
    band = rz[0]
    for k in hops:
        band = band + rz[k]
    bc[...] = band
    bslot = lambda i: band_ref.at[urow(i)]
    b2 = gather(2, bc, bslot, False)
    band_ref[urow(r)] = band
    gp[...] = -mul(split(band), (vh[...], vl[...]), NT)
    g0 = col_stage(4, lambda p: gp, gr.at[c])
    gr[c] = gp[...]
    arrive(t0)
    total = rt[0]
    for i in range(1, nc):
        total = total + rt[i]
    few = each // nr
    for i in range(nr):
        st[i] = total[i * few : (i + 1) * few]
    t1 = row_stage(6, lambda p: st.at[p], tt.at[r])
    tt[r] = st[r]
    b2[0]()
    b2[1]()
    arrive(g0)
    total = gr[0]
    for i in range(1, nc):
        total = total + gr[i]
    gc[...] = total
    cslot = lambda i: both_ref.at[urow(i)]
    g1 = gather(3, gc, cslot, True)
    both_ref[urow(r)] = total
    arrive(t1)
    total = tt[0]
    for i in range(1, nr):
        total = total + tt[i]
    gt[r] = total
    t2 = row_stage(7, lambda p: gt.at[r], gt.at[r])
    b2[2]()
    g1[0]()
    g1[1]()
    arrive(p0)
    strip = rp[0]
    for i in range(1, nc):
        strip = strip + rp[i]
    strip_ref[...] = strip
    arrive(t2)
    tslot = lambda i: top_ref.at[i]
    t3 = spread_start(5, gt, tslot)
    top_ref[c] = gt[...]
    g1[2]()
    arrive(spread_end(5, t3, tslot))
    b2[3]()
    g1[3]()
    for copy in sent:
        copy.wait_send()


def finish(strip_ref, band_ref, both_ref, top_ref, corner, top, bottom, left, right, sem):
    width = top_ref.shape[0]
    pairs = (
        (band_ref, right), (strip_ref, bottom), (top_ref, top),
        (both_ref.at[:, pl.ds(0, width)], corner), (both_ref.at[:, pl.ds(width, width)], left),
    )
    copies = [pltpu.make_async_copy(source, target, sem.at[i]) for i, (source, target) in enumerate(pairs)]
    for copy in copies:
        copy.start()
    for copy in copies:
        copy.wait()


def body(an, ln, un, lot, lo, uol, uo, dln, dun, iln, iun, dlo, duo, ilo, iuo):
    nr, nc = lax.axis_size("row"), lax.axis_size("col")
    rows, cols = an.shape
    width = iln.shape[0]
    hu, wl, each = width // nr, rows // nc, width // nc
    ny = nc // 2 if nc % 2 == 0 and nr % max(nc // 2, 1) == 0 else 1
    nz = nr // ny
    vm = pl.BlockSpec(memory_space=pltpu.VMEM)
    hbm = pl.BlockSpec(memory_space=pltpu.HBM)
    V, D = pltpu.VMEM, pltpu.SemaphoreType.DMA
    lanes = max(nr, 3 + (2 + nz) * ny)
    whole = V((nr, each // nr, width), f32)
    operands = (an, un, uo, ln.T, lo.T, lot, uol, iln, iun, ilo, iuo)
    strip, band, both, top = pl.pallas_call(
        functools.partial(kernel, nr, nc, ny),
        out_shape=(
            V((wl, width), f32), V((width, cols), f32), V((width, 2 * width), f32), V((nc, nr, each // nr, width), f32)
        ),
        in_specs=[hbm] * 11,
        out_specs=(vm, vm, vm, vm),
        scratch_shapes=[
            V((rows, cols), f32), V((rows, cols), bf16), V((rows, cols), bf16),
            V((2, nr, hu, cols), f32), V((2, nc, each, rows), f32),
            V((2 * width, cols), bf16), V((2 * width, cols), bf16),
            V((width, cols), f32), V((rows, width), f32),
            V((nz, ny, hu, cols), f32), V((nz, hu, cols), f32), V((nz, hu, cols), f32),
            V((nc, wl, width), f32), V((hu, cols), f32),
            V((hu, 2 * width), f32), V((nc, hu, 2 * width), f32), V((hu, 2 * width), f32),
            V((width, width), f32), V((nc, each, width), f32), whole, whole, whole,
            V((6, width, width), f32),
            D, D((6,)), D((4,)), D((8, lanes)), D((8, lanes)), D((6, nc)), D((6, nc)),
        ],
        compiler_params=pltpu.CompilerParams(collective_id=0, has_side_effects=True, vmem_limit_bytes=LIMIT),
    )(*[pltpu.with_memory_space_constraint(v, pltpu.HBM) for v in operands])
    shapes = [(width, width), (width, width), strip.shape, (width, width), band.shape]
    return pl.pallas_call(
        finish,
        out_shape=[jax.ShapeDtypeStruct(shape, f32) for shape in shapes],
        in_specs=[vm] * 4,
        out_specs=[hbm] * 5,
        scratch_shapes=[D((5,))],
        compiler_params=pltpu.CompilerParams(vmem_limit_bytes=1 << 20),
    )(strip, band, both, top.reshape(width, width))


def solution(mesh):
    two, whole = P("row", "col"), P()
    return jax.shard_map(
        body,
        mesh=mesh,
        in_specs=(two, two, two, whole, two, whole, two) + (whole,) * 8,
        out_specs=(P(), P(), P(("row", "col"), None), P(), P(None, "col")),
        check_vma=False,
    )
```

```python
import functools

import jax
import jax.numpy as jnp
from jax import lax
from jax.experimental import pallas as pl
from jax.experimental.pallas import tpu as pltpu
from jax.sharding import PartitionSpec as P

f32, bf16 = jnp.float32, jnp.bfloat16
NN, NT = ((1,), (0,)), ((1,), (1,))
LIMIT = 48 << 20


def split(x):
    high = x.astype(bf16)
    return high, (x - high.astype(f32)).astype(bf16)


def mul(a, b, dims=NN):
    def one(x, y):
        return lax.dot_general(x, y, (dims, ((), ())), preferred_element_type=f32)

    return one(a[0], b[0]) + (one(a[0], b[1]) + one(a[1], b[0]))


def flip(z, k):
    bit = 1
    while bit <= k:
        if k & bit:
            z = z + bit - 2 * bit * lax.rem(z // bit, 2)
        bit *= 2
    return z


def arrive(copies):
    for copy in copies:
        copy.wait_recv()


def kernel(
    nr, nc, ny, a_hbm, un_hbm, uo_hbm, ln_hbm, lo_hbm, lot_hbm, uol_hbm, iln_hbm, iun_hbm, ilo_hbm, iuo_hbm,
    strip_ref, band_ref, both_ref, top_ref,
    a_ref, ah, al, xu, xl, vh, vl, pb, ps, ry, sz, rz, fp, tp, rp, bc, gp, gn, gr, gc,
    pt, nt, ft, rt, st, tt, gt, sq,
    asem, qsem, osem, rs_send, rs_recv, cs_send, cs_recv,
):
    r, c = lax.axis_index("row"), lax.axis_index("col")
    rows, cols = a_hbm.shape
    wl = rows // nc
    width = iln_hbm.shape[0]
    hu = width // nr
    nz = nr // ny
    z, y = r // ny, lax.rem(r, ny)
    even = nz & (nz - 1) == 0
    hops = list(range(1, nz))
    reach = lambda k: flip(z, k) if even else lax.rem(z + k, nz)
    origin = lambda k: flip(z, k) if even else lax.rem(z - k + nz, nz)
    cores = 2
    nx = nc // cores
    x, core = c // cores, lax.rem(c, cores)

    load = pltpu.make_async_copy(a_hbm, a_ref, asem)
    squares = (iuo_hbm, uol_hbm, iun_hbm, iln_hbm, lot_hbm, ilo_hbm)
    loads = [pltpu.make_async_copy(m, sq.at[i], qsem.at[i]) for i, m in enumerate(squares)]
    own = [
        pltpu.make_async_copy(source, target, osem.at[i])
        for i, (source, target) in enumerate(
            [(un_hbm, xu.at[0, r]), (uo_hbm, xu.at[1, r]), (ln_hbm, xl.at[0, c]), (lo_hbm, xl.at[1, c])]
        )
    ]
    for copy in loads + own:
        copy.start()
    load.start()
    barrier = pltpu.get_barrier_semaphore()
    for d in range(1, nr):
        pl.semaphore_signal(barrier, inc=1, device_id={"row": lax.rem(r + d, nr)}, device_id_type=pl.DeviceIdType.MESH)
    for d in range(1, nc):
        pl.semaphore_signal(barrier, inc=1, device_id={"col": lax.rem(c + d, nc)}, device_id_type=pl.DeviceIdType.MESH)
    pl.semaphore_wait(barrier, nr + nc - 2)

    def lrow(i):
        return pl.ds(pl.multiple_of(i * wl, wl), wl)

    def urow(i):
        return pl.ds(pl.multiple_of(i * hu, hu), hu)

    sent = []

    def put(axis, peer, source, target, send, recv):
        copy = pltpu.make_async_remote_copy(
            src_ref=source,
            dst_ref=target,
            send_sem=send,
            recv_sem=recv,
            device_id={axis: peer},
            device_id_type=pl.DeviceIdType.MESH,
        )
        copy.start()
        sent.append(copy)
        return copy

    def push(stage, index, source, target, peer):
        return put("row", peer, source, target, rs_send.at[stage, index], rs_recv.at[stage, index])

    def toss(stage, index, source, target, peer):
        return put("col", peer, source, target, cs_send.at[stage, index], cs_recv.at[stage, index])

    quad = nz == 4

    def across(stage, k, zk, slot, source=None):
        here = slot(zk * ny + y)
        base = 3 + 2 * ny + k * ny
        source = here if source is None else source
        return [push(stage, base + d, source, here, z * ny + lax.rem(y + d, ny)) for d in range(1, ny)]

    def gather(stage, source, slot, flat):
        here = slot(r)
        near = lambda i, chunk, origin=None: push(
            stage, i, slot(chunk) if origin is None else origin, slot(chunk), flip(z, 1) * ny + y
        )
        over = across(stage, 0, z, slot, source)
        if not quad:
            along = [push(stage, k, source, here, reach(k) * ny + y) for k in hops]

            def relay(k):
                def step():
                    along[k - 1].wait_recv()
                    over.extend(across(stage, k, origin(k), slot))

                return step

            steps = [relay(k) for k in hops]
            return steps + [lambda: None] * (3 - len(steps)) + [lambda: arrive(over)]
        far = push(stage, 1, source, here, flip(z, 2) * ny + y)
        first = near(0, r, source)
        ends, mid = [], []

        def one():
            if flat:
                arrive(over)
                for d in range(1, ny):
                    ends.append(near(2 + d, z * ny + lax.rem(y - d + ny, ny)))
            else:
                first.wait_recv()
                over.extend(across(stage, 1, flip(z, 1), slot))

        def two():
            far.wait_recv()
            mid.append(near(2, flip(z, 2) * ny + y))
            (ends if flat else over).extend(across(stage, 2, flip(z, 2), slot))

        def three():
            if flat:
                arrive(ends[ny - 1 :])
                for d in range(1, ny):
                    mid.append(near(2 + ny + d, flip(z, 2) * ny + lax.rem(y - d + ny, ny)))
            else:
                arrive(mid)
                over.extend(across(stage, 3, flip(z, 3), slot))

        def four():
            arrive([first] + ends[: ny - 1] + mid if flat else over)

        return [one, two, three, four]

    other = x * cores + 1 - core

    def twin(stage, k, source, target):
        return [toss(stage, nx + k, source, target, other)]

    def spread_start(stage, source, slot):
        along = [toss(stage, k, source, slot(c), lax.rem(x + k, nx) * cores + core) for k in range(1, nx)]
        return along, twin(stage, 0, source, slot(c))

    def spread_end(stage, state, slot):
        along, near = state
        for k in range(1, nx):
            along[k - 1].wait_recv()
            here = slot(lax.rem(x - k + nx, nx) * cores + core)
            near = near + twin(stage, k, here, here)
        return near

    def row_stage(stage, source, target):
        peers = [lax.rem(r + d, nr) for d in range(1, nr)]
        return [push(stage, d, source(p), target, p) for d, p in enumerate(peers, 1)]

    def fold_near(stage, block, got):
        return [toss(stage, q, block(q * cores + 1 - core), got.at[q], other) for q in range(nx)]

    def fold_far(stage, copies, block, near, send, got):
        arrive(copies)
        out = []
        for k in [*range(1, nx), 0]:
            q = lax.rem(x + k, nx)
            total = block(q * cores + core)[...] + near[q]
            if k:
                send[k] = total
                out.append(toss(stage, nx + k, send.at[k], got.at[k], q * cores + core))
            else:
                got[0] = total
        return out

    def fold_end(copies, got):
        arrive(copies)
        total = got[0]
        for k in range(1, nx):
            total = total + got[k]
        return total

    lslot = [lambda i: xl.at[0, i], lambda i: xl.at[1, i]]
    uslot = [lambda i: xu.at[0, i], lambda i: xu.at[1, i]]
    low = [spread_start(0, ln_hbm, lslot[0]), spread_start(1, lo_hbm, lslot[1])]
    up = [gather(0, un_hbm, uslot[0], False), gather(1, uo_hbm, uslot[1], True)]
    for copy in own + loads:
        copy.wait()
    iuo, iun = split(sq[0]), split(sq[2])
    mix_u = split(mul(split(mul(iuo, split(sq[1]))), iun))
    ilo = sq[5]
    mix_l = mul(split(mul(split(sq[3]), split(sq[4]))), split(ilo))
    mix_l, ilo, iln = split(mix_l.T), split(ilo.T), split(sq[3].T)
    load.wait()
    high, rest = split(a_ref[...])
    ah[...] = high
    al[...] = rest
    up[0][0]()
    up[1][0]()
    up[0][1]()
    near = spread_end(0, low[0], lslot[0])
    near = near + spread_end(1, low[1], lslot[1])
    arrive(near)
    ln, lo = split(xl[0].reshape(width, rows)), split(xl[1].reshape(width, rows))
    lts = split(mul(ilo, lo) - mul(mix_l, ln))
    lns = split(mul(iln, ln))
    for i in range(cols // width):
        here = slice(i * width, (i + 1) * width)
        pb[:, here] = -mul(lts, (ah[:, here], al[:, here]))
    up[1][1]()
    up[0][2]()
    b0 = {}
    for k in hops[::-1] + [0]:
        zt = reach(k) if k else z
        peers = [zt * ny + lax.rem(y + d, ny) for d in range(1, ny)]
        b0[k] = [
            push(4, k * ny + d, pb.at[urow(p)], ry.at[k, d], z * ny + lax.rem(y + d, ny)) for d, p in enumerate(peers, 1)
        ]
    b1 = {}
    for k in hops[::-1] + [0]:
        arrive(b0[k])
        zt = reach(k) if k else z
        total = pb[urow(zt * ny + y)]
        for d in range(1, ny):
            total = total + ry[k, d]
        if k:
            sz[k] = total
            b1[k] = push(5, k, sz.at[k], rz.at[k], zt * ny + y)
        else:
            rz[0] = total
        if k == hops[-1]:
            up[1][2]()
    up[0][3]()
    up[1][3]()
    for i in range(cols // width):
        here = slice(i * width, (i + 1) * width)
        un, uo = split(xu[0, :, :, here].reshape(width, width)), split(xu[1, :, :, here].reshape(width, width))
        vh[:width, here], vl[:width, here] = split(mul(iuo, uo) - mul(mix_u, un))
        vh[width:, here], vl[width:, here] = split(mul(iun, un))
    for i in range(rows // width):
        here = slice(i * width, (i + 1) * width)
        ps[here] = -mul((ah[here], al[here]), (vh[:width], vl[:width]), NT)
    pt[...] = -mul(lns, split(ps[...]))
    each = width // nc
    part = lambda p: pt.at[pl.ds(pl.multiple_of(p * each, each), each)]
    piece = lambda p: ps.at[lrow(p)]
    t0 = fold_near(3, part, nt)
    t0 = fold_far(3, t0, part, nt, ft, rt)
    arrive([b1[k] for k in hops])
    band = rz[0]
    for k in hops:
        band = band + rz[k]
    bc[...] = band
    bslot = lambda i: band_ref.at[urow(i)]
    b2 = gather(2, bc, bslot, False)
    band_ref[urow(r)] = band
    gp[...] = -mul(split(band), (vh[...], vl[...]), NT)
    half = lambda i: gp.at[:, pl.ds(pl.multiple_of(i * width, width), width)]
    g0 = [toss(4, 0, half(1 - core), gn, other)]
    p0 = fold_near(2, piece, fp)
    arrive(g0)
    mine = half(core)[...] + gn[...]
    gr[0] = mine
    g0 = [toss(4, k, gr.at[0], gr.at[k], lax.rem(x + k, nx) * cores + core) for k in range(1, nx)]
    p0 = fold_far(2, p0, piece, fp, tp, rp)
    total = fold_end(t0, rt)
    few = each // nr
    for i in range(nr):
        st[i] = total[i * few : (i + 1) * few]
    t1 = row_stage(6, lambda p: st.at[p], tt.at[r])
    tt[r] = st[r]
    b2[0]()
    b2[1]()
    total = fold_end(g0, gr)
    gc[...] = total
    cslot = lambda i: both_ref.at[core, urow(i)]
    g1 = gather(3, gc, cslot, True)
    both_ref[core, urow(r)] = total
    arrive(t1)
    total = tt[0]
    for i in range(1, nr):
        total = total + tt[i]
    gt[r] = total
    t2 = row_stage(7, lambda p: gt.at[r], gt.at[r])
    b2[2]()
    g1[0]()
    g1[1]()
    strip_ref[...] = fold_end(p0, rp)
    arrive(t2)
    tslot = lambda i: top_ref.at[i]
    t3 = spread_start(5, gt, tslot)
    top_ref[c] = gt[...]
    g1[2]()
    g1[3]()
    g2 = toss(4, nx, both_ref.at[core], both_ref.at[core], other)
    t3 = spread_end(5, t3, tslot)
    b2[3]()
    arrive(t3)
    arrive([g2])
    for copy in sent:
        copy.wait_send()


def finish(strip_ref, band_ref, both_ref, top_ref, corner, top, bottom, left, right, sem):
    pairs = (
        (band_ref, right), (strip_ref, bottom), (top_ref, top),
        (both_ref.at[0], corner), (both_ref.at[1], left),
    )
    copies = [pltpu.make_async_copy(source, target, sem.at[i]) for i, (source, target) in enumerate(pairs)]
    for copy in copies:
        copy.start()
    for copy in copies:
        copy.wait()


def body(an, ln, un, lot, lo, uol, uo, dln, dun, iln, iun, dlo, duo, ilo, iuo):
    nr, nc = lax.axis_size("row"), lax.axis_size("col")
    rows, cols = an.shape
    width = iln.shape[0]
    hu, wl, each = width // nr, rows // nc, width // nc
    ny = nc // 2 if nr % (nc // 2) == 0 else 1
    nz = nr // ny
    vm = pl.BlockSpec(memory_space=pltpu.VMEM)
    hbm = pl.BlockSpec(memory_space=pltpu.HBM)
    V, D = pltpu.VMEM, pltpu.SemaphoreType.DMA
    lanes = max(nr, 3 + (2 + nz) * ny)
    whole = V((nr, each // nr, width), f32)
    operands = (an, un, uo, ln.T, lo.T, lot, uol, iln, iun, ilo, iuo)
    strip, band, both, top = pl.pallas_call(
        functools.partial(kernel, nr, nc, ny),
        out_shape=(
            V((wl, width), f32), V((width, cols), f32), V((2, width, width), f32), V((nc, nr, each // nr, width), f32)
        ),
        in_specs=[hbm] * 11,
        out_specs=(vm, vm, vm, vm),
        scratch_shapes=[
            V((rows, cols), f32), V((rows, cols), bf16), V((rows, cols), bf16),
            V((2, nr, hu, cols), f32), V((2, nc, each, rows), f32),
            V((2 * width, cols), bf16), V((2 * width, cols), bf16),
            V((width, cols), f32), V((rows, width), f32),
            V((nz, ny, hu, cols), f32), V((nz, hu, cols), f32), V((nz, hu, cols), f32),
            *[V((nc // 2, wl, width), f32)] * 3, V((hu, cols), f32),
            V((hu, 2 * width), f32), V((hu, width), f32), V((nc // 2, hu, width), f32), V((hu, width), f32),
            V((width, width), f32), *[V((nc // 2, each, width), f32)] * 3, whole, whole, whole,
            V((6, width, width), f32),
            D, D((6,)), D((4,)), D((8, lanes)), D((8, lanes)), D((6, nc)), D((6, nc)),
        ],
        compiler_params=pltpu.CompilerParams(collective_id=0, has_side_effects=True, vmem_limit_bytes=LIMIT),
    )(*[pltpu.with_memory_space_constraint(v, pltpu.HBM) for v in operands])
    shapes = [(width, width), (width, width), strip.shape, (width, width), band.shape]
    return pl.pallas_call(
        finish,
        out_shape=[jax.ShapeDtypeStruct(shape, f32) for shape in shapes],
        in_specs=[vm] * 4,
        out_specs=[hbm] * 5,
        scratch_shapes=[D((5,))],
        compiler_params=pltpu.CompilerParams(vmem_limit_bytes=1 << 20),
    )(strip, band, both, top.reshape(width, width))


def solution(mesh):
    two, whole = P("row", "col"), P()
    return jax.shard_map(
        body,
        mesh=mesh,
        in_specs=(two, two, two, whole, two, whole, two) + (whole,) * 8,
        out_specs=(P(), P(), P(("row", "col"), None), P(), P(None, "col")),
        check_vma=False,
    )
```

```python
import functools

import jax
import jax.numpy as jnp
from jax import lax
from jax.experimental import pallas as pl
from jax.experimental.pallas import tpu as pltpu
from jax.sharding import PartitionSpec as P

f32, bf16 = jnp.float32, jnp.bfloat16
NN, NT = ((1,), (0,)), ((1,), (1,))
LIMIT = 48 << 20


def split(x):
    high = x.astype(bf16)
    return high, (x - high.astype(f32)).astype(bf16)


def mul(a, b, dims=NN):
    def one(x, y):
        return lax.dot_general(x, y, (dims, ((), ())), preferred_element_type=f32)

    return one(a[0], b[0]) + (one(a[0], b[1]) + one(a[1], b[0]))


def flip(z, k):
    bit = 1
    while bit <= k:
        if k & bit:
            z = z + bit - 2 * bit * lax.rem(z // bit, 2)
        bit *= 2
    return z


def arrive(copies):
    for copy in copies:
        copy.wait_recv()


def kernel(
    nr, nc, ny, a_hbm, un_hbm, uo_hbm, ln_hbm, lo_hbm, lot_hbm, uol_hbm, iln_hbm, iun_hbm, ilo_hbm, iuo_hbm,
    strip_ref, band_ref, both_ref, top_ref,
    a_ref, ah, al, xu, xl, vh, vl, pb, ps, ry, sz, rz, fp, tp, rp, bc, gp, gn, gr, gc,
    pt, nt, ft, rt, st, tt, gt, sq,
    asem, qsem, osem, rs_send, rs_recv, cs_send, cs_recv,
):
    r, c = lax.axis_index("row"), lax.axis_index("col")
    rows, cols = a_hbm.shape
    wl = rows // nc
    width = iln_hbm.shape[0]
    hu = width // nr
    nz = nr // ny
    z, y = r // ny, lax.rem(r, ny)
    even = nz & (nz - 1) == 0
    hops = list(range(1, nz))
    reach = lambda k: flip(z, k) if even else lax.rem(z + k, nz)
    origin = lambda k: flip(z, k) if even else lax.rem(z - k + nz, nz)
    cores = 2
    nx = nc // cores
    x, core = c // cores, lax.rem(c, cores)

    load = pltpu.make_async_copy(a_hbm, a_ref, asem)
    squares = (iuo_hbm, uol_hbm, iun_hbm, iln_hbm, lot_hbm, ilo_hbm)
    loads = [pltpu.make_async_copy(m, sq.at[i], qsem.at[i]) for i, m in enumerate(squares)]
    own = [
        pltpu.make_async_copy(source, target, osem.at[i])
        for i, (source, target) in enumerate(
            [(un_hbm, xu.at[0, r]), (uo_hbm, xu.at[1, r]), (ln_hbm, xl.at[0, c]), (lo_hbm, xl.at[1, c])]
        )
    ]
    for copy in loads + own:
        copy.start()
    load.start()
    barrier = pltpu.get_barrier_semaphore()
    for d in range(1, nr):
        pl.semaphore_signal(barrier, inc=1, device_id={"row": lax.rem(r + d, nr)}, device_id_type=pl.DeviceIdType.MESH)
    for d in range(1, nc):
        pl.semaphore_signal(barrier, inc=1, device_id={"col": lax.rem(c + d, nc)}, device_id_type=pl.DeviceIdType.MESH)
    pl.semaphore_wait(barrier, nr + nc - 2)

    def lrow(i):
        return pl.ds(pl.multiple_of(i * wl, wl), wl)

    def urow(i):
        return pl.ds(pl.multiple_of(i * hu, hu), hu)

    sent = []

    def put(axis, peer, source, target, send, recv):
        copy = pltpu.make_async_remote_copy(
            src_ref=source,
            dst_ref=target,
            send_sem=send,
            recv_sem=recv,
            device_id={axis: peer},
            device_id_type=pl.DeviceIdType.MESH,
        )
        copy.start()
        sent.append(copy)
        return copy

    def push(stage, index, source, target, peer):
        return put("row", peer, source, target, rs_send.at[stage, index], rs_recv.at[stage, index])

    def toss(stage, index, source, target, peer):
        return put("col", peer, source, target, cs_send.at[stage, index], cs_recv.at[stage, index])

    quad = nz == 4

    def across(stage, k, zk, slot, source=None):
        here = slot(zk * ny + y)
        base = 3 + 2 * ny + k * ny
        source = here if source is None else source
        return [push(stage, base + d, source, here, z * ny + lax.rem(y + d, ny)) for d in range(1, ny)]

    def gather(stage, source, slot, flat):
        here = slot(r)
        near = lambda i, chunk, origin=None: push(
            stage, i, slot(chunk) if origin is None else origin, slot(chunk), flip(z, 1) * ny + y
        )
        over = across(stage, 0, z, slot, source)
        if not quad:
            along = [push(stage, k, source, here, reach(k) * ny + y) for k in hops]

            def relay(k):
                def step():
                    along[k - 1].wait_recv()
                    over.extend(across(stage, k, origin(k), slot))

                return step

            steps = [relay(k) for k in hops]
            return steps + [lambda: None] * (3 - len(steps)) + [lambda: arrive(over)]
        far = push(stage, 1, source, here, flip(z, 2) * ny + y)
        first = near(0, r, source)
        ends, mid = [], []

        def one():
            if flat:
                arrive(over)
                for d in range(1, ny):
                    ends.append(near(2 + d, z * ny + lax.rem(y - d + ny, ny)))
            else:
                first.wait_recv()
                over.extend(across(stage, 1, flip(z, 1), slot))

        def two():
            far.wait_recv()
            mid.append(near(2, flip(z, 2) * ny + y))
            (ends if flat else over).extend(across(stage, 2, flip(z, 2), slot))

        def three():
            if flat:
                arrive(ends[ny - 1 :])
                for d in range(1, ny):
                    mid.append(near(2 + ny + d, flip(z, 2) * ny + lax.rem(y - d + ny, ny)))
            else:
                arrive(mid)
                over.extend(across(stage, 3, flip(z, 3), slot))

        def four():
            arrive([first] + ends[: ny - 1] + mid if flat else over)

        return [one, two, three, four]

    other = x * cores + 1 - core

    def twin(stage, k, source, target):
        return [toss(stage, nx + k, source, target, other)]

    def spread_start(stage, source, slot):
        along = [toss(stage, k, source, slot(c), lax.rem(x + k, nx) * cores + core) for k in range(1, nx)]
        return along, twin(stage, 0, source, slot(c))

    def spread_end(stage, state, slot):
        along, near = state
        for k in range(1, nx):
            along[k - 1].wait_recv()
            here = slot(lax.rem(x - k + nx, nx) * cores + core)
            near = near + twin(stage, k, here, here)
        return near

    def row_stage(stage, source, target):
        peers = [lax.rem(r + d, nr) for d in range(1, nr)]
        return [push(stage, d, source(p), target, p) for d, p in enumerate(peers, 1)]

    def fold_near(stage, block, got):
        return [toss(stage, q, block(q * cores + 1 - core), got.at[q], other) for q in range(nx)]

    def fold_far(stage, copies, block, near, send, got):
        arrive(copies)
        out = []
        for k in [*range(1, nx), 0]:
            q = lax.rem(x + k, nx)
            total = block(q * cores + core)[...] + near[q]
            if k:
                send[k] = total
                out.append(toss(stage, nx + k, send.at[k], got.at[k], q * cores + core))
            else:
                got[0] = total
        return out

    def fold_end(copies, got):
        arrive(copies)
        total = got[0]
        for k in range(1, nx):
            total = total + got[k]
        return total

    lslot = [lambda i: xl.at[0, i], lambda i: xl.at[1, i]]
    uslot = [lambda i: xu.at[0, i], lambda i: xu.at[1, i]]
    low = [spread_start(0, ln_hbm, lslot[0]), spread_start(1, lo_hbm, lslot[1])]
    up = [gather(0, un_hbm, uslot[0], False), gather(1, uo_hbm, uslot[1], True)]
    for copy in own + loads:
        copy.wait()
    iuo, iun = split(sq[0]), split(sq[2])
    mix_u = split(mul(split(mul(iuo, split(sq[1]))), iun))
    ilo = sq[5]
    mix_l = mul(split(mul(split(sq[3]), split(sq[4]))), split(ilo))
    mix_l, ilo, iln = split(mix_l.T), split(ilo.T), split(sq[3].T)
    load.wait()
    high, rest = split(a_ref[...])
    ah[...] = high
    al[...] = rest
    up[0][0]()
    up[1][0]()
    up[0][1]()
    near = spread_end(0, low[0], lslot[0])
    near = near + spread_end(1, low[1], lslot[1])
    arrive(near)
    ln, lo = split(xl[0].reshape(width, rows)), split(xl[1].reshape(width, rows))
    lts = split(mul(ilo, lo) - mul(mix_l, ln))
    lns = split(mul(iln, ln))
    for i in range(cols // width):
        here = slice(i * width, (i + 1) * width)
        pb[:, here] = -mul(lts, (ah[:, here], al[:, here]))
    b0 = {}
    for k in hops[::-1] + [0]:
        zt = reach(k) if k else z
        peers = [zt * ny + lax.rem(y + d, ny) for d in range(1, ny)]
        b0[k] = [
            push(4, k * ny + d, pb.at[urow(p)], ry.at[k, d], z * ny + lax.rem(y + d, ny)) for d, p in enumerate(peers, 1)
        ]
    up[1][1]()
    up[0][2]()
    b1 = {}
    for k in hops[::-1] + [0]:
        arrive(b0[k])
        zt = reach(k) if k else z
        total = pb[urow(zt * ny + y)]
        for d in range(1, ny):
            total = total + ry[k, d]
        if k:
            sz[k] = total
            b1[k] = push(5, k, sz.at[k], rz.at[k], zt * ny + y)
        else:
            rz[0] = total
        if k == hops[-1]:
            up[1][2]()
    up[0][3]()
    up[1][3]()
    for i in range(cols // width):
        here = slice(i * width, (i + 1) * width)
        un, uo = split(xu[0, :, :, here].reshape(width, width)), split(xu[1, :, :, here].reshape(width, width))
        vh[:width, here], vl[:width, here] = split(mul(iuo, uo) - mul(mix_u, un))
        vh[width:, here], vl[width:, here] = split(mul(iun, un))
    for i in range(rows // width):
        here = slice(i * width, (i + 1) * width)
        ps[here] = -mul((ah[here], al[here]), (vh[:width], vl[:width]), NT)
    pt[...] = -mul(lns, split(ps[...]))
    each = width // nc
    part = lambda p: pt.at[pl.ds(pl.multiple_of(p * each, each), each)]
    piece = lambda p: ps.at[lrow(p)]
    t0 = fold_near(3, part, nt)
    t0 = fold_far(3, t0, part, nt, ft, rt)
    arrive([b1[k] for k in hops])
    band = rz[0]
    for k in hops:
        band = band + rz[k]
    bc[...] = band
    bslot = lambda i: band_ref.at[urow(i)]
    b2 = gather(2, bc, bslot, False)
    band_ref[urow(r)] = band
    gp[...] = -mul(split(band), (vh[...], vl[...]), NT)
    half = lambda i: gp.at[:, pl.ds(pl.multiple_of(i * width, width), width)]
    g0 = [toss(4, 0, half(1 - core), gn, other)]
    p0 = fold_near(2, piece, fp)
    arrive(g0)
    mine = half(core)[...] + gn[...]
    gr[0] = mine
    g0 = [toss(4, k, gr.at[0], gr.at[k], lax.rem(x + k, nx) * cores + core) for k in range(1, nx)]
    p0 = fold_far(2, p0, piece, fp, tp, rp)
    total = fold_end(t0, rt)
    few = each // nr
    for i in range(nr):
        st[i] = total[i * few : (i + 1) * few]
    t1 = row_stage(6, lambda p: st.at[p], tt.at[r])
    tt[r] = st[r]
    total = fold_end(g0, gr)
    gc[...] = total
    cslot = lambda i: both_ref.at[core, urow(i)]
    g1 = gather(3, gc, cslot, True)
    both_ref[core, urow(r)] = total
    b2[0]()
    b2[1]()
    arrive(t1)
    total = tt[0]
    for i in range(1, nr):
        total = total + tt[i]
    gt[r] = total
    t2 = row_stage(7, lambda p: gt.at[r], gt.at[r])
    g1[0]()
    g1[1]()
    b2[2]()
    g1[2]()
    strip_ref[...] = fold_end(p0, rp)
    arrive(t2)
    tslot = lambda i: top_ref.at[i]
    t3 = spread_start(5, gt, tslot)
    top_ref[c] = gt[...]
    g1[3]()
    g2 = toss(4, nx, both_ref.at[core], both_ref.at[core], other)
    t3 = spread_end(5, t3, tslot)
    b2[3]()
    arrive(t3)
    arrive([g2])
    for copy in sent:
        copy.wait_send()


def finish(strip_ref, band_ref, both_ref, top_ref, corner, top, bottom, left, right, sem):
    pairs = (
        (band_ref, right), (strip_ref, bottom), (top_ref, top),
        (both_ref.at[0], corner), (both_ref.at[1], left),
    )
    copies = [pltpu.make_async_copy(source, target, sem.at[i]) for i, (source, target) in enumerate(pairs)]
    for copy in copies:
        copy.start()
    for copy in copies:
        copy.wait()


def body(an, ln, un, lot, lo, uol, uo, dln, dun, iln, iun, dlo, duo, ilo, iuo):
    nr, nc = lax.axis_size("row"), lax.axis_size("col")
    rows, cols = an.shape
    width = iln.shape[0]
    hu, wl, each = width // nr, rows // nc, width // nc
    ny = nc // 2 if nr % (nc // 2) == 0 else 1
    nz = nr // ny
    vm = pl.BlockSpec(memory_space=pltpu.VMEM)
    hbm = pl.BlockSpec(memory_space=pltpu.HBM)
    V, D = pltpu.VMEM, pltpu.SemaphoreType.DMA
    lanes = max(nr, 3 + (2 + nz) * ny)
    whole = V((nr, each // nr, width), f32)
    operands = (an, un, uo, ln.T, lo.T, lot, uol, iln, iun, ilo, iuo)
    strip, band, both, top = pl.pallas_call(
        functools.partial(kernel, nr, nc, ny),
        out_shape=(
            V((wl, width), f32), V((width, cols), f32), V((2, width, width), f32), V((nc, nr, each // nr, width), f32)
        ),
        in_specs=[hbm] * 11,
        out_specs=(vm, vm, vm, vm),
        scratch_shapes=[
            V((rows, cols), f32), V((rows, cols), bf16), V((rows, cols), bf16),
            V((2, nr, hu, cols), f32), V((2, nc, each, rows), f32),
            V((2 * width, cols), bf16), V((2 * width, cols), bf16),
            V((width, cols), f32), V((rows, width), f32),
            V((nz, ny, hu, cols), f32), V((nz, hu, cols), f32), V((nz, hu, cols), f32),
            *[V((nc // 2, wl, width), f32)] * 3, V((hu, cols), f32),
            V((hu, 2 * width), f32), V((hu, width), f32), V((nc // 2, hu, width), f32), V((hu, width), f32),
            V((width, width), f32), *[V((nc // 2, each, width), f32)] * 3, whole, whole, whole,
            V((6, width, width), f32),
            D, D((6,)), D((4,)), D((8, lanes)), D((8, lanes)), D((6, nc)), D((6, nc)),
        ],
        compiler_params=pltpu.CompilerParams(collective_id=0, has_side_effects=True, vmem_limit_bytes=LIMIT),
    )(*[pltpu.with_memory_space_constraint(v, pltpu.HBM) for v in operands])
    shapes = [(width, width), (width, width), strip.shape, (width, width), band.shape]
    return pl.pallas_call(
        finish,
        out_shape=[jax.ShapeDtypeStruct(shape, f32) for shape in shapes],
        in_specs=[vm] * 4,
        out_specs=[hbm] * 5,
        scratch_shapes=[D((5,))],
        compiler_params=pltpu.CompilerParams(vmem_limit_bytes=1 << 20),
    )(strip, band, both, top.reshape(width, width))


def solution(mesh):
    two, whole = P("row", "col"), P()
    return jax.shard_map(
        body,
        mesh=mesh,
        in_specs=(two, two, two, whole, two, whole, two) + (whole,) * 8,
        out_specs=(P(), P(), P(("row", "col"), None), P(), P(None, "col")),
        check_vma=False,
    )
```

```python
import functools

import jax
import jax.numpy as jnp
from jax import lax
from jax.experimental import pallas as pl
from jax.experimental.pallas import tpu as pltpu
from jax.sharding import PartitionSpec as P

f32, bf16 = jnp.float32, jnp.bfloat16
NN, NT = ((1,), (0,)), ((1,), (1,))
LIMIT = 48 << 20


def split(x):
    high = x.astype(bf16)
    return high, (x - high.astype(f32)).astype(bf16)


def mul(a, b, dims=NN):
    def one(x, y):
        return lax.dot_general(x, y, (dims, ((), ())), preferred_element_type=f32)

    return one(a[0], b[0]) + (one(a[0], b[1]) + one(a[1], b[0]))


def flip(z, k):
    bit = 1
    while bit <= k:
        if k & bit:
            z = z + bit - 2 * bit * lax.rem(z // bit, 2)
        bit *= 2
    return z


def arrive(copies):
    for copy in copies:
        copy.wait_recv()


def kernel(
    nr, nc, ny, a_hbm, un_hbm, uo_hbm, ln_hbm, lo_hbm, lot_hbm, uol_hbm, iln_hbm, iun_hbm, ilo_hbm, iuo_hbm,
    strip_ref, band_ref, both_ref, top_ref,
    a_ref, ah, al, xu, xl, vh, vl, pb, ps, ry, sz, rz, fp, tp, rp, bc, gp, gn, gr, gc,
    pt, nt, st, tt, sq,
    asem, qsem, osem, rs_send, rs_recv, cs_send, cs_recv, ws_send, ws_recv,
):
    r, c = lax.axis_index("row"), lax.axis_index("col")
    rows, cols = a_hbm.shape
    wl = rows // nc
    width = iln_hbm.shape[0]
    hu = width // nr
    nz = nr // ny
    z, y = r // ny, lax.rem(r, ny)
    even = nz & (nz - 1) == 0
    hops = list(range(1, nz))
    reach = lambda k: flip(z, k) if even else lax.rem(z + k, nz)
    origin = lambda k: flip(z, k) if even else lax.rem(z - k + nz, nz)
    cores = 2
    nx = nc // cores
    x, core = c // cores, lax.rem(c, cores)

    load = pltpu.make_async_copy(a_hbm, a_ref, asem)
    squares = (iuo_hbm, uol_hbm, iun_hbm, iln_hbm, lot_hbm, ilo_hbm)
    loads = [pltpu.make_async_copy(m, sq.at[i], qsem.at[i]) for i, m in enumerate(squares)]
    own = [
        pltpu.make_async_copy(source, target, osem.at[i])
        for i, (source, target) in enumerate(
            [(un_hbm, xu.at[0, r]), (uo_hbm, xu.at[1, r]), (ln_hbm, xl.at[0, c]), (lo_hbm, xl.at[1, c])]
        )
    ]
    for copy in loads + own:
        copy.start()
    load.start()
    barrier = pltpu.get_barrier_semaphore()
    for d in range(1, nr):
        pl.semaphore_signal(barrier, inc=1, device_id={"row": lax.rem(r + d, nr)}, device_id_type=pl.DeviceIdType.MESH)
    for d in range(1, nc):
        pl.semaphore_signal(barrier, inc=1, device_id={"col": lax.rem(c + d, nc)}, device_id_type=pl.DeviceIdType.MESH)
    pl.semaphore_wait(barrier, nr + nc - 2)

    def lrow(i):
        return pl.ds(pl.multiple_of(i * wl, wl), wl)

    def urow(i):
        return pl.ds(pl.multiple_of(i * hu, hu), hu)

    sent = []

    def put(axis, peer, source, target, send, recv):
        copy = pltpu.make_async_remote_copy(
            src_ref=source,
            dst_ref=target,
            send_sem=send,
            recv_sem=recv,
            device_id=peer if axis is None else {axis: peer},
            device_id_type=pl.DeviceIdType.MESH,
        )
        copy.start()
        sent.append(copy)
        return copy

    def push(stage, index, source, target, peer):
        return put("row", peer, source, target, rs_send.at[stage, index], rs_recv.at[stage, index])

    def toss(stage, index, source, target, peer):
        return put("col", peer, source, target, cs_send.at[stage, index], cs_recv.at[stage, index])

    quad = nz == 4

    def across(stage, k, zk, slot, source=None):
        here = slot(zk * ny + y)
        base = 3 + 2 * ny + k * ny
        source = here if source is None else source
        return [push(stage, base + d, source, here, z * ny + lax.rem(y + d, ny)) for d in range(1, ny)]

    def gather(stage, source, slot, flat):
        here = slot(r)
        near = lambda i, chunk, origin=None: push(
            stage, i, slot(chunk) if origin is None else origin, slot(chunk), flip(z, 1) * ny + y
        )
        over = across(stage, 0, z, slot, source)
        if not quad:
            along = [push(stage, k, source, here, reach(k) * ny + y) for k in hops]

            def relay(k):
                def step():
                    along[k - 1].wait_recv()
                    over.extend(across(stage, k, origin(k), slot))

                return step

            steps = [relay(k) for k in hops]
            return steps + [lambda: None] * (3 - len(steps)) + [lambda: arrive(over)]
        far = push(stage, 1, source, here, flip(z, 2) * ny + y)
        first = near(0, r, source)
        ends, mid = [], []

        def one():
            if flat:
                arrive(over)
                for d in range(1, ny):
                    ends.append(near(2 + d, z * ny + lax.rem(y - d + ny, ny)))
            else:
                first.wait_recv()
                over.extend(across(stage, 1, flip(z, 1), slot))

        def two():
            far.wait_recv()
            mid.append(near(2, flip(z, 2) * ny + y))
            (ends if flat else over).extend(across(stage, 2, flip(z, 2), slot))

        def three():
            if flat:
                arrive(ends[ny - 1 :])
                for d in range(1, ny):
                    mid.append(near(2 + ny + d, flip(z, 2) * ny + lax.rem(y - d + ny, ny)))
            else:
                arrive(mid)
                over.extend(across(stage, 3, flip(z, 3), slot))

        def four():
            arrive([first] + ends[: ny - 1] + mid if flat else over)

        return [one, two, three, four]

    other = x * cores + 1 - core

    def twin(stage, k, source, target):
        return [toss(stage, nx + k, source, target, other)]

    def spread_start(stage, source, slot):
        along = [toss(stage, k, source, slot(c), lax.rem(x + k, nx) * cores + core) for k in range(1, nx)]
        return along, twin(stage, 0, source, slot(c))

    def spread_end(stage, state, slot):
        along, near = state
        for k in range(1, nx):
            along[k - 1].wait_recv()
            here = slot(lax.rem(x - k + nx, nx) * cores + core)
            near = near + twin(stage, k, here, here)
        return near

    def row_stage(stage, source, target):
        peers = [lax.rem(r + d, nr) for d in range(1, nr)]
        return [push(stage, d, source(p), target, p) for d, p in enumerate(peers, 1)]

    def fold_near(stage, block, got):
        return [toss(stage, q, block(q * cores + 1 - core), got.at[q], other) for q in range(nx)]

    def fold_far(stage, copies, block, near, send, got):
        arrive(copies)
        out = []
        for k in [*range(1, nx), 0]:
            q = lax.rem(x + k, nx)
            total = block(q * cores + core)[...] + near[q]
            if k:
                send[k] = total
                out.append(toss(stage, nx + k, send.at[k], got.at[k], q * cores + core))
            else:
                got[0] = total
        return out

    def fold_end(copies, got):
        arrive(copies)
        total = got[0]
        for k in range(1, nx):
            total = total + got[k]
        return total

    lslot = [lambda i: xl.at[0, i], lambda i: xl.at[1, i]]
    uslot = [lambda i: xu.at[0, i], lambda i: xu.at[1, i]]
    low = [spread_start(0, ln_hbm, lslot[0]), spread_start(1, lo_hbm, lslot[1])]
    up = [gather(0, un_hbm, uslot[0], False), gather(1, uo_hbm, uslot[1], True)]
    for copy in own + loads:
        copy.wait()
    iuo, iun = split(sq[0]), split(sq[2])
    mix_u = split(mul(split(mul(iuo, split(sq[1]))), iun))
    ilo = sq[5]
    mix_l = mul(split(mul(split(sq[3]), split(sq[4]))), split(ilo))
    mix_l, ilo, iln = split(mix_l.T), split(ilo.T), split(sq[3].T)
    load.wait()
    high, rest = split(a_ref[...])
    ah[...] = high
    al[...] = rest
    q = {}
    b0, b1 = {}, {}
    each, few = width // nc, width // nc // nr
    part = lambda p: pt.at[pl.ds(pl.multiple_of(p * each, each), each)]
    piece = lambda p: ps.at[lrow(p)]
    half = lambda i: gp.at[:, pl.ds(pl.multiple_of(i * width, width), width)]
    cslot = lambda i: both_ref.at[core, urow(i)]

    def lower():
        near = spread_end(0, low[0], lslot[0])
        near = near + spread_end(1, low[1], lslot[1])
        arrive(near)
        ln, lo = split(xl[0].reshape(width, rows)), split(xl[1].reshape(width, rows))
        lts = split(mul(ilo, lo) - mul(mix_l, ln))
        q["lns"] = split(mul(iln, ln))
        for i in range(cols // width):
            here = slice(i * width, (i + 1) * width)
            pb[:, here] = -mul(lts, (ah[:, here], al[:, here]))

    def spill(k):
        zt = reach(k) if k else z
        peers = [zt * ny + lax.rem(y + d, ny) for d in range(1, ny)]
        b0[k] = [
            push(4, k * ny + d, pb.at[urow(p)], ry.at[k, d], z * ny + lax.rem(y + d, ny)) for d, p in enumerate(peers, 1)
        ]

    def pile(k):
        arrive(b0[k])
        zt = reach(k) if k else z
        total = pb[urow(zt * ny + y)]
        for d in range(1, ny):
            total = total + ry[k, d]
        if k:
            sz[k] = total
            b1[k] = push(5, k, sz.at[k], rz.at[k], zt * ny + y)
        else:
            rz[0] = total

    def upper():
        for i in range(cols // width):
            here = slice(i * width, (i + 1) * width)
            un, uo = split(xu[0, :, :, here].reshape(width, width)), split(xu[1, :, :, here].reshape(width, width))
            vh[:width, here], vl[:width, here] = split(mul(iuo, uo) - mul(mix_u, un))
            vh[width:, here], vl[width:, here] = split(mul(iun, un))
        for i in range(rows // width):
            here = slice(i * width, (i + 1) * width)
            ps[here] = -mul((ah[here], al[here]), (vh[:width], vl[:width]), NT)
        pt[...] = -mul(q["lns"], split(ps[...]))
        q["t0"] = fold_near(3, part, nt)

    def wide(stage, source, target):
        out = []
        for n in range(1, nx * nr):
            qx, p = lax.rem(x + n // nr, nx), lax.rem(r + n % nr, nr)
            peer = {"row": p, "col": qx * cores + core}
            out.append(put(None, peer, source(qx, p), target, ws_send.at[stage, n], ws_recv.at[stage, n]))
        return out

    def top_far():
        arrive(q["t0"])
        for i in range(nx):
            total = part(i * cores + core)[...] + nt[i]
            for k in range(nr):
                st[i, k] = total[k * few : (k + 1) * few]
        q["t1"] = wide(0, lambda i, p: st.at[i, p], tt.at[x, r])
        tt[x, r] = st[x, r]

    def band():
        arrive([b1[k] for k in hops])
        total = rz[0]
        for k in hops:
            total = total + rz[k]
        bc[...] = total
        band_ref[urow(r)] = total
        q["b"] = gather(2, bc, lambda i: band_ref.at[urow(i)], False)

    def inner():
        gp[...] = -mul(split(bc[...]), (vh[...], vl[...]), NT)
        q["g0"] = [toss(4, 0, half(1 - core), gn, other)]
        q["p0"] = fold_near(2, piece, fp)

    def inner_far():
        arrive(q["g0"])
        gr[0] = half(core)[...] + gn[...]
        q["g0"] = [toss(4, k, gr.at[0], gr.at[k], lax.rem(x + k, nx) * cores + core) for k in range(1, nx)]

    def strip_far():
        q["p0"] = fold_far(2, q["p0"], piece, fp, tp, rp)

    def inner_row():
        total = fold_end(q["g0"], gr)
        gc[...] = total
        both_ref[core, urow(r)] = total
        q["g"] = row_stage(3, lambda p: gc, cslot(r))

    def top_back():
        arrive(q["t1"])
        total = None
        for i in range(nx):
            for k in range(nr):
                total = tt[i, k] if total is None else total + tt[i, k]
        top_ref[c, r] = total
        q["t2"] = wide(1, lambda i, p: top_ref.at[c, r], top_ref.at[c, r])

    def top_twin():
        arrive(q["t2"])
        mine = [top_ref.at[i * cores + core] for i in range(nx)]
        q["t3"] = [toss(3, nx + i, ref, ref, other) for i, ref in enumerate(mine)]

    def strip_end():
        strip_ref[...] = fold_end(q["p0"], rp)

    def swap():
        arrive(q["g"])
        q["g2"] = toss(4, nx, both_ref.at[core], both_ref.at[core], other)

    far_first = hops[::-1] + [0]
    up[0][0]()
    up[1][0]()
    up[0][1]()
    lower()
    for k in far_first:
        spill(k)
    up[1][1]()
    for k in far_first[:1]:
        pile(k)
    up[0][2]()
    for k in far_first[1:]:
        pile(k)
    up[1][2]()
    up[0][3]()
    up[1][3]()
    band()
    upper()
    top_far()
    inner()
    inner_far()
    strip_far()
    q["b"][0]()
    q["b"][1]()
    inner_row()
    top_back()
    q["b"][2]()
    top_twin()
    swap()
    strip_end()
    q["b"][3]()
    arrive(q["t3"])
    arrive([q["g2"]])
    for copy in sent:
        copy.wait_send()


def finish(strip_ref, band_ref, both_ref, top_ref, corner, top, bottom, left, right, sem):
    pairs = (
        (band_ref, right), (strip_ref, bottom), (top_ref, top),
        (both_ref.at[0], corner), (both_ref.at[1], left),
    )
    copies = [pltpu.make_async_copy(source, target, sem.at[i]) for i, (source, target) in enumerate(pairs)]
    for copy in copies:
        copy.start()
    for copy in copies:
        copy.wait()


def body(an, ln, un, lot, lo, uol, uo, dln, dun, iln, iun, dlo, duo, ilo, iuo):
    nr, nc = lax.axis_size("row"), lax.axis_size("col")
    rows, cols = an.shape
    width = iln.shape[0]
    hu, wl, each = width // nr, rows // nc, width // nc
    ny = nc // 2 if nr % (nc // 2) == 0 else 1
    nz = nr // ny
    vm = pl.BlockSpec(memory_space=pltpu.VMEM)
    hbm = pl.BlockSpec(memory_space=pltpu.HBM)
    V, D = pltpu.VMEM, pltpu.SemaphoreType.DMA
    lanes = max(nr, 3 + (2 + nz) * ny)
    whole = V((nc // 2, nr, each // nr, width), f32)
    operands = (an, un, uo, ln.T, lo.T, lot, uol, iln, iun, ilo, iuo)
    strip, band, both, top = pl.pallas_call(
        functools.partial(kernel, nr, nc, ny),
        out_shape=(
            V((wl, width), f32), V((width, cols), f32), V((2, width, width), f32), V((nc, nr, each // nr, width), f32)
        ),
        in_specs=[hbm] * 11,
        out_specs=(vm, vm, vm, vm),
        scratch_shapes=[
            V((rows, cols), f32), V((rows, cols), bf16), V((rows, cols), bf16),
            V((2, nr, hu, cols), f32), V((2, nc, each, rows), f32),
            V((2 * width, cols), bf16), V((2 * width, cols), bf16),
            V((width, cols), f32), V((rows, width), f32),
            V((nz, ny, hu, cols), f32), V((nz, hu, cols), f32), V((nz, hu, cols), f32),
            *[V((nc // 2, wl, width), f32)] * 3, V((hu, cols), f32),
            V((hu, 2 * width), f32), V((hu, width), f32), V((nc // 2, hu, width), f32), V((hu, width), f32),
            V((width, width), f32), V((nc // 2, each, width), f32), whole, whole,
            V((6, width, width), f32),
            D, D((6,)), D((4,)), D((6, lanes)), D((6, lanes)), D((6, nc)), D((6, nc)), D((2, nc // 2 * nr)), D((2, nc // 2 * nr)),
        ],
        compiler_params=pltpu.CompilerParams(collective_id=0, has_side_effects=True, vmem_limit_bytes=LIMIT),
    )(*[pltpu.with_memory_space_constraint(v, pltpu.HBM) for v in operands])
    shapes = [(width, width), (width, width), strip.shape, (width, width), band.shape]
    return pl.pallas_call(
        finish,
        out_shape=[jax.ShapeDtypeStruct(shape, f32) for shape in shapes],
        in_specs=[vm] * 4,
        out_specs=[hbm] * 5,
        scratch_shapes=[D((5,))],
        compiler_params=pltpu.CompilerParams(vmem_limit_bytes=1 << 20),
    )(strip, band, both, top.reshape(width, width))


def solution(mesh):
    two, whole = P("row", "col"), P()
    return jax.shard_map(
        body,
        mesh=mesh,
        in_specs=(two, two, two, whole, two, whole, two) + (whole,) * 8,
        out_specs=(P(), P(), P(("row", "col"), None), P(), P(None, "col")),
        check_vma=False,
    )
```

```python
import functools

import jax
import jax.numpy as jnp
from jax import lax
from jax.experimental import pallas as pl
from jax.experimental.pallas import tpu as pltpu
from jax.sharding import PartitionSpec as P

f32, bf16 = jnp.float32, jnp.bfloat16
NN, NT = ((1,), (0,)), ((1,), (1,))
LIMIT = 48 << 20


def split(x):
    high = x.astype(bf16)
    return high, (x - high.astype(f32)).astype(bf16)


def mul(a, b, dims=NN):
    def one(x, y):
        return lax.dot_general(x, y, (dims, ((), ())), preferred_element_type=f32)

    return one(a[0], b[0]) + (one(a[0], b[1]) + one(a[1], b[0]))


def flip(z, k):
    bit = 1
    while bit <= k:
        if k & bit:
            z = z + bit - 2 * bit * lax.rem(z // bit, 2)
        bit *= 2
    return z


def arrive(copies):
    for copy in copies:
        copy.wait_recv()


def kernel(
    nr, nc, ny, a_hbm, un_hbm, uo_hbm, ln_hbm, lo_hbm, lot_hbm, uol_hbm, iln_hbm, iun_hbm, ilo_hbm, iuo_hbm,
    strip_ref, band_ref, both_ref, top_ref,
    a_ref, ah, al, xu, xl, vh, vl, pb, ps, ry, sz, rz, fp, tp, rp, bc, gp, gn, gr, gc,
    pt, nt, st, tt, sq,
    asem, qsem, osem, rs_send, rs_recv, cs_send, cs_recv, ws_send, ws_recv, ready,
):
    r, c = lax.axis_index("row"), lax.axis_index("col")
    rows, cols = a_hbm.shape
    wl = rows // nc
    width = iln_hbm.shape[0]
    hu = width // nr
    nz = nr // ny
    z, y = r // ny, lax.rem(r, ny)
    even = nz & (nz - 1) == 0
    hops = list(range(1, nz))
    reach = lambda k: flip(z, k) if even else lax.rem(z + k, nz)
    origin = lambda k: flip(z, k) if even else lax.rem(z - k + nz, nz)
    cores = 2
    nx = nc // cores
    x, core = c // cores, lax.rem(c, cores)

    load = pltpu.make_async_copy(a_hbm, a_ref, asem)
    squares = (iuo_hbm, uol_hbm, iun_hbm, iln_hbm, lot_hbm, ilo_hbm)
    loads = [pltpu.make_async_copy(m, sq.at[i], qsem.at[i]) for i, m in enumerate(squares)]
    own = [
        pltpu.make_async_copy(source, target, osem.at[i])
        for i, (source, target) in enumerate(
            [(un_hbm, xu.at[0, r]), (uo_hbm, xu.at[1, r]), (ln_hbm, xl.at[0, c]), (lo_hbm, xl.at[1, c])]
        )
    ]
    for copy in loads + own:
        copy.start()
    load.start()
    barrier = pltpu.get_barrier_semaphore()
    friends = [{"row": reach(k) * ny + y} for k in ((1, 2) if nz == 4 else hops)]
    friends += [{"row": z * ny + lax.rem(y + d, ny)} for d in range(1, ny)]
    friends += [{"col": x * cores + 1 - core}] + [{"col": lax.rem(x + k, nx) * cores + core} for k in range(1, nx)]
    for friend in friends:
        pl.semaphore_signal(barrier, inc=1, device_id=friend, device_id_type=pl.DeviceIdType.MESH)
    pl.semaphore_wait(barrier, len(friends))

    def lrow(i):
        return pl.ds(pl.multiple_of(i * wl, wl), wl)

    def urow(i):
        return pl.ds(pl.multiple_of(i * hu, hu), hu)

    sent = []

    def put(axis, peer, source, target, send, recv):
        copy = pltpu.make_async_remote_copy(
            src_ref=source,
            dst_ref=target,
            send_sem=send,
            recv_sem=recv,
            device_id=peer if axis is None else {axis: peer},
            device_id_type=pl.DeviceIdType.MESH,
        )
        copy.start()
        sent.append(copy)
        return copy

    def push(stage, index, source, target, peer):
        return put("row", peer, source, target, rs_send.at[stage, index], rs_recv.at[stage, index])

    def toss(stage, index, source, target, peer):
        return put("col", peer, source, target, cs_send.at[stage, index], cs_recv.at[stage, index])

    quad = nz == 4

    def across(stage, k, zk, slot, source=None):
        here = slot(zk * ny + y)
        base = 3 + 2 * ny + k * ny
        source = here if source is None else source
        return [push(stage, base + d, source, here, z * ny + lax.rem(y + d, ny)) for d in range(1, ny)]

    def gather(stage, source, slot, flat):
        here = slot(r)
        near = lambda i, chunk, origin=None: push(
            stage, i, slot(chunk) if origin is None else origin, slot(chunk), flip(z, 1) * ny + y
        )
        over = across(stage, 0, z, slot, source)
        if not quad:
            along = [push(stage, k, source, here, reach(k) * ny + y) for k in hops]

            def relay(k):
                def step():
                    along[k - 1].wait_recv()
                    over.extend(across(stage, k, origin(k), slot))

                return step

            steps = [relay(k) for k in hops]
            return steps + [lambda: None] * (3 - len(steps)) + [lambda: arrive(over)]
        far = push(stage, 1, source, here, flip(z, 2) * ny + y)
        first = near(0, r, source)
        ends, mid = [], []

        def one():
            if flat:
                arrive(over)
                for d in range(1, ny):
                    ends.append(near(2 + d, z * ny + lax.rem(y - d + ny, ny)))
            else:
                first.wait_recv()
                over.extend(across(stage, 1, flip(z, 1), slot))

        def two():
            far.wait_recv()
            mid.append(near(2, flip(z, 2) * ny + y))
            (ends if flat else over).extend(across(stage, 2, flip(z, 2), slot))

        def three():
            if flat:
                arrive(ends[ny - 1 :])
                for d in range(1, ny):
                    mid.append(near(2 + ny + d, flip(z, 2) * ny + lax.rem(y - d + ny, ny)))
            else:
                arrive(mid)
                over.extend(across(stage, 3, flip(z, 3), slot))

        def four():
            arrive([first] + ends[: ny - 1] + mid if flat else over)

        return [one, two, three, four]

    other = x * cores + 1 - core

    def twin(stage, k, source, target):
        return [toss(stage, nx + k, source, target, other)]

    def spread_start(stage, source, slot):
        along = [toss(stage, k, source, slot(c), lax.rem(x + k, nx) * cores + core) for k in range(1, nx)]
        return along, twin(stage, 0, source, slot(c))

    def spread_end(stage, state, slot):
        along, near = state
        for k in range(1, nx):
            along[k - 1].wait_recv()
            here = slot(lax.rem(x - k + nx, nx) * cores + core)
            near = near + twin(stage, k, here, here)
        return near

    def row_stage(stage, source, target):
        peers = [lax.rem(r + d, nr) for d in range(1, nr)]
        return [push(stage, d, source(p), target, p) for d, p in enumerate(peers, 1)]

    def fold_near(stage, block, got):
        return [toss(stage, q, block(q * cores + 1 - core), got.at[q], other) for q in range(nx)]

    def fold_far(stage, copies, block, near, send, got):
        arrive(copies)
        out = []
        for k in [*range(1, nx), 0]:
            q = lax.rem(x + k, nx)
            total = block(q * cores + core)[...] + near[q]
            if k:
                send[k] = total
                out.append(toss(stage, nx + k, send.at[k], got.at[k], q * cores + core))
            else:
                got[0] = total
        return out

    def fold_end(copies, got):
        arrive(copies)
        total = got[0]
        for k in range(1, nx):
            total = total + got[k]
        return total

    lslot = [lambda i: xl.at[0, i], lambda i: xl.at[1, i]]
    uslot = [lambda i: xu.at[0, i], lambda i: xu.at[1, i]]
    low = [spread_start(0, ln_hbm, lslot[0]), spread_start(1, lo_hbm, lslot[1])]
    up = [gather(0, un_hbm, uslot[0], False), gather(1, uo_hbm, uslot[1], True)]
    for copy in own + loads:
        copy.wait()
    iuo, iun = split(sq[0]), split(sq[2])
    mix_u = split(mul(split(mul(iuo, split(sq[1]))), iun))
    ilo = sq[5]
    mix_l = mul(split(mul(split(sq[3]), split(sq[4]))), split(ilo))
    mix_l, ilo, iln = split(mix_l.T), split(ilo.T), split(sq[3].T)
    load.wait()
    high, rest = split(a_ref[...])
    ah[...] = high
    al[...] = rest
    q = {}
    b0, b1 = {}, {}
    each, few = width // nc, width // nc // nr
    part = lambda p: pt.at[pl.ds(pl.multiple_of(p * each, each), each)]
    piece = lambda p: ps.at[lrow(p)]
    half = lambda i: gp.at[:, pl.ds(pl.multiple_of(i * width, width), width)]
    cslot = lambda i: both_ref.at[core, urow(i)]

    def lower():
        near = spread_end(0, low[0], lslot[0])
        near = near + spread_end(1, low[1], lslot[1])
        arrive(near)
        ln, lo = split(xl[0].reshape(width, rows)), split(xl[1].reshape(width, rows))
        lts = split(mul(ilo, lo) - mul(mix_l, ln))
        q["lns"] = split(mul(iln, ln))
        for i in range(cols // width):
            here = slice(i * width, (i + 1) * width)
            pb[:, here] = -mul(lts, (ah[:, here], al[:, here]))

    def spill(k):
        zt = reach(k) if k else z
        peers = [zt * ny + lax.rem(y + d, ny) for d in range(1, ny)]
        b0[k] = [
            push(4, k * ny + d, pb.at[urow(p)], ry.at[k, d], z * ny + lax.rem(y + d, ny))
            for d, p in enumerate(peers, 1)
        ]

    def pile(k):
        arrive(b0[k])
        zt = reach(k) if k else z
        total = pb[urow(zt * ny + y)]
        for d in range(1, ny):
            total = total + ry[k, d]
        if k:
            sz[k] = total
            b1[k] = push(5, k, sz.at[k], rz.at[k], zt * ny + y)
        else:
            rz[0] = total

    def band():
        arrive([b1[k] for k in hops])
        total = rz[0]
        for k in hops:
            total = total + rz[k]
        bc[...] = total
        band_ref[urow(r)] = total
        q["b"] = gather(2, bc, lambda i: band_ref.at[urow(i)], False)

    def upper():
        for i in range(cols // width):
            here = slice(i * width, (i + 1) * width)
            un, uo = split(xu[0, :, :, here].reshape(width, width)), split(xu[1, :, :, here].reshape(width, width))
            vh[:width, here], vl[:width, here] = split(mul(iuo, uo) - mul(mix_u, un))
        for i in range(rows // width):
            here = slice(i * width, (i + 1) * width)
            ps[here] = -mul((ah[here], al[here]), (vh[:width], vl[:width]), NT)
        pt[...] = -mul(q["lns"], split(ps[...]))
        q["t0"] = fold_near(3, part, nt)
        for i in range(cols // width):
            here = slice(i * width, (i + 1) * width)
            un = split(xu[0, :, :, here].reshape(width, width))
            vh[width:, here], vl[width:, here] = split(mul(iun, un))

    def wide(stage, source, target):
        out = []
        for n in range(1, nx * nr):
            qx, p = lax.rem(x + n // nr, nx), lax.rem(r + n % nr, nr)
            peer = {"row": p, "col": qx * cores + core}
            out.append(put(None, peer, source(qx, p), target, ws_send.at[stage, n], ws_recv.at[stage, n]))
        return out

    def tell():
        for k in range(1, nx):
            peer = lax.rem(x + k, nx) * cores + core
            pl.semaphore_signal(ready, inc=1, device_id={"col": peer}, device_id_type=pl.DeviceIdType.MESH)

    def top_far():
        pl.semaphore_wait(ready, nx - 1)
        arrive(q["t0"])
        for i in range(nx):
            total = part(i * cores + core)[...] + nt[i]
            for k in range(nr):
                st[i, k] = total[k * few : (k + 1) * few]
        q["t1"] = wide(0, lambda i, p: st.at[i, p], tt.at[x, r])
        tt[x, r] = st[x, r]

    def inner():
        gp[...] = -mul(split(bc[...]), (vh[...], vl[...]), NT)
        q["g0"] = [toss(4, 0, half(1 - core), gn, other)]
        q["p0"] = fold_near(2, piece, fp)

    def inner_far():
        arrive(q["g0"])
        gr[0] = half(core)[...] + gn[...]
        q["g0"] = [toss(4, k, gr.at[0], gr.at[k], lax.rem(x + k, nx) * cores + core) for k in range(1, nx)]

    def strip_far():
        q["p0"] = fold_far(2, q["p0"], piece, fp, tp, rp)

    def inner_row():
        total = fold_end(q["g0"], gr)
        gc[...] = total
        both_ref[core, urow(r)] = total
        q["g"] = row_stage(3, lambda p: gc, cslot(r))

    def top_back():
        arrive(q["t1"])
        total = None
        for i in range(nx):
            for k in range(nr):
                total = tt[i, k] if total is None else total + tt[i, k]
        top_ref[c, r] = total
        q["t2"] = wide(1, lambda i, p: top_ref.at[c, r], top_ref.at[c, r])

    def top_twin():
        arrive(q["t2"])
        mine = [top_ref.at[i * cores + core] for i in range(nx)]
        q["t3"] = [toss(3, nx + i, ref, ref, other) for i, ref in enumerate(mine)]

    def strip_end():
        strip_ref[...] = fold_end(q["p0"], rp)

    def swap():
        arrive(q["g"])
        q["g2"] = toss(4, nx, both_ref.at[core], both_ref.at[core], other)

    far_first = hops[::-1] + [0]
    up[0][0]()
    up[1][0]()
    up[0][1]()
    lower()
    for k in far_first:
        spill(k)
    up[1][1]()
    for k in far_first[:1]:
        pile(k)
    up[0][2]()
    for k in far_first[1:]:
        pile(k)
    up[1][2]()
    up[0][3]()
    up[1][3]()
    tell()
    band()
    upper()
    top_far()
    inner()
    inner_far()
    strip_far()
    q["b"][0]()
    q["b"][1]()
    inner_row()
    top_back()
    q["b"][2]()
    top_twin()
    swap()
    strip_end()
    q["b"][3]()
    arrive(q["t3"])
    arrive([q["g2"]])
    for copy in sent:
        copy.wait_send()


def finish(strip_ref, band_ref, both_ref, top_ref, corner, top, bottom, left, right, sem):
    pairs = (
        (band_ref, right), (strip_ref, bottom), (top_ref, top),
        (both_ref.at[0], corner), (both_ref.at[1], left),
    )
    copies = [pltpu.make_async_copy(source, target, sem.at[i]) for i, (source, target) in enumerate(pairs)]
    for copy in copies:
        copy.start()
    for copy in copies:
        copy.wait()


def body(an, ln, un, lot, lo, uol, uo, dln, dun, iln, iun, dlo, duo, ilo, iuo):
    nr, nc = lax.axis_size("row"), lax.axis_size("col")
    rows, cols = an.shape
    width = iln.shape[0]
    hu, wl, each = width // nr, rows // nc, width // nc
    ny = nc // 2 if nr % (nc // 2) == 0 else 1
    nz = nr // ny
    vm = pl.BlockSpec(memory_space=pltpu.VMEM)
    hbm = pl.BlockSpec(memory_space=pltpu.HBM)
    V, D = pltpu.VMEM, pltpu.SemaphoreType.DMA
    lanes = max(nr, 3 + (2 + nz) * ny)
    whole = V((nc // 2, nr, each // nr, width), f32)
    operands = (an, un, uo, ln.T, lo.T, lot, uol, iln, iun, ilo, iuo)
    strip, band, both, top = pl.pallas_call(
        functools.partial(kernel, nr, nc, ny),
        out_shape=(
            V((wl, width), f32), V((width, cols), f32), V((2, width, width), f32), V((nc, nr, each // nr, width), f32)
        ),
        in_specs=[hbm] * 11,
        out_specs=(vm, vm, vm, vm),
        scratch_shapes=[
            V((rows, cols), f32), V((rows, cols), bf16), V((rows, cols), bf16),
            V((2, nr, hu, cols), f32), V((2, nc, each, rows), f32),
            V((2 * width, cols), bf16), V((2 * width, cols), bf16),
            V((width, cols), f32), V((rows, width), f32),
            V((nz, ny, hu, cols), f32), V((nz, hu, cols), f32), V((nz, hu, cols), f32),
            *[V((nc // 2, wl, width), f32)] * 3, V((hu, cols), f32),
            V((hu, 2 * width), f32), V((hu, width), f32), V((nc // 2, hu, width), f32), V((hu, width), f32),
            V((width, width), f32), V((nc // 2, each, width), f32), whole, whole,
            V((6, width, width), f32),
            D, D((6,)), D((4,)), D((6, lanes)), D((6, lanes)), D((6, nc)), D((6, nc)), D((2, nc // 2 * nr)), D((2, nc // 2 * nr)), pltpu.SemaphoreType.REGULAR,
        ],
        compiler_params=pltpu.CompilerParams(collective_id=0, has_side_effects=True, vmem_limit_bytes=LIMIT),
    )(*[pltpu.with_memory_space_constraint(v, pltpu.HBM) for v in operands])
    shapes = [(width, width), (width, width), strip.shape, (width, width), band.shape]
    return pl.pallas_call(
        finish,
        out_shape=[jax.ShapeDtypeStruct(shape, f32) for shape in shapes],
        in_specs=[vm] * 4,
        out_specs=[hbm] * 5,
        scratch_shapes=[D((5,))],
        compiler_params=pltpu.CompilerParams(vmem_limit_bytes=1 << 20),
    )(strip, band, both, top.reshape(width, width))


def solution(mesh):
    two, whole = P("row", "col"), P()
    return jax.shard_map(
        body,
        mesh=mesh,
        in_specs=(two, two, two, whole, two, whole, two) + (whole,) * 8,
        out_specs=(P(), P(), P(("row", "col"), None), P(), P(None, "col")),
        check_vma=False,
    )
```

```python
import functools

import jax
import jax.numpy as jnp
from jax import lax
from jax.experimental import pallas as pl
from jax.experimental.pallas import tpu as pltpu
from jax.sharding import PartitionSpec as P

f32, bf16 = jnp.float32, jnp.bfloat16
NN, NT = ((1,), (0,)), ((1,), (1,))
LIMIT = 48 << 20


def split(x):
    high = x.astype(bf16)
    return high, (x - high.astype(f32)).astype(bf16)


def mul(a, b, dims=NN):
    def one(x, y):
        return lax.dot_general(x, y, (dims, ((), ())), preferred_element_type=f32)

    return one(a[0], b[0]) + (one(a[0], b[1]) + one(a[1], b[0]))


def flip(z, k):
    bit = 1
    while bit <= k:
        if k & bit:
            z = z + bit - 2 * bit * lax.rem(z // bit, 2)
        bit *= 2
    return z


def arrive(copies):
    for copy in copies:
        copy.wait_recv()


def kernel(
    nr, nc, ny, a_hbm, un_hbm, uo_hbm, ln_hbm, lo_hbm, lot_hbm, uol_hbm, iln_hbm, iun_hbm, ilo_hbm, iuo_hbm,
    strip_ref, band_ref, both_ref, top_ref,
    a_ref, ah, al, xu, xl, vh, vl, pb, ps, ry, sz, rz, fp, tp, rp, bc, gp, gn, gr, gc,
    pt, nt, st, tt, sq,
    asem, qsem, osem, rs_send, rs_recv, cs_send, cs_recv, ws_send, ws_recv, ready,
):
    r, c = lax.axis_index("row"), lax.axis_index("col")
    rows, cols = a_hbm.shape
    wl = rows // nc
    width = iln_hbm.shape[0]
    hu = width // nr
    nz = nr // ny
    z, y = r // ny, lax.rem(r, ny)
    even = nz & (nz - 1) == 0
    hops = list(range(1, nz))
    reach = lambda k: flip(z, k) if even else lax.rem(z + k, nz)
    origin = lambda k: flip(z, k) if even else lax.rem(z - k + nz, nz)
    cores = 2
    nx = nc // cores
    x, core = c // cores, lax.rem(c, cores)

    load = pltpu.make_async_copy(a_hbm, a_ref, asem)
    squares = (iuo_hbm, uol_hbm, iun_hbm, iln_hbm, lot_hbm, ilo_hbm)
    loads = [pltpu.make_async_copy(m, sq.at[i], qsem.at[i]) for i, m in enumerate(squares)]
    own = [
        pltpu.make_async_copy(source, target, osem.at[i])
        for i, (source, target) in enumerate(
            [(un_hbm, xu.at[0, r]), (uo_hbm, xu.at[1, r]), (ln_hbm, xl.at[0, c]), (lo_hbm, xl.at[1, c])]
        )
    ]
    for copy in own + loads:
        copy.start()
    load.start()
    barrier = pltpu.get_barrier_semaphore()
    friends = [{"row": reach(k) * ny + y} for k in ((1, 2) if nz == 4 else hops)]
    friends += [{"row": z * ny + lax.rem(y + d, ny)} for d in range(1, ny)]
    friends += [{"col": x * cores + 1 - core}] + [{"col": lax.rem(x + k, nx) * cores + core} for k in range(1, nx)]
    for friend in friends:
        pl.semaphore_signal(barrier, inc=1, device_id=friend, device_id_type=pl.DeviceIdType.MESH)
    pl.semaphore_wait(barrier, len(friends))

    def lrow(i):
        return pl.ds(pl.multiple_of(i * wl, wl), wl)

    def urow(i):
        return pl.ds(pl.multiple_of(i * hu, hu), hu)

    sent = []

    def put(axis, peer, source, target, send, recv):
        copy = pltpu.make_async_remote_copy(
            src_ref=source,
            dst_ref=target,
            send_sem=send,
            recv_sem=recv,
            device_id=peer if axis is None else {axis: peer},
            device_id_type=pl.DeviceIdType.MESH,
        )
        copy.start()
        sent.append(copy)
        return copy

    def push(stage, index, source, target, peer):
        return put("row", peer, source, target, rs_send.at[stage, index], rs_recv.at[stage, index])

    def toss(stage, index, source, target, peer):
        return put("col", peer, source, target, cs_send.at[stage, index], cs_recv.at[stage, index])

    quad = nz == 4

    def across(stage, k, zk, slot, source=None):
        here = slot(zk * ny + y)
        base = 3 + 2 * ny + k * ny
        source = here if source is None else source
        return [push(stage, base + d, source, here, z * ny + lax.rem(y + d, ny)) for d in range(1, ny)]

    def gather(stage, source, slot, flat):
        here = slot(r)
        near = lambda i, chunk, origin=None: push(
            stage, i, slot(chunk) if origin is None else origin, slot(chunk), flip(z, 1) * ny + y
        )
        over = across(stage, 0, z, slot, source)
        if not quad:
            along = [push(stage, k, source, here, reach(k) * ny + y) for k in hops]

            def relay(k):
                def step():
                    along[k - 1].wait_recv()
                    over.extend(across(stage, k, origin(k), slot))

                return step

            steps = [relay(k) for k in hops]
            return steps + [lambda: None] * (3 - len(steps)) + [lambda: arrive(over)]
        far = push(stage, 1, source, here, flip(z, 2) * ny + y)
        first = near(0, r, source)
        ends, mid = [], []

        def one():
            if flat:
                arrive(over)
                for d in range(1, ny):
                    ends.append(near(2 + d, z * ny + lax.rem(y - d + ny, ny)))
            else:
                first.wait_recv()
                over.extend(across(stage, 1, flip(z, 1), slot))

        def two():
            far.wait_recv()
            mid.append(near(2, flip(z, 2) * ny + y))
            (ends if flat else over).extend(across(stage, 2, flip(z, 2), slot))

        def three():
            if flat:
                arrive(ends[ny - 1 :])
                for d in range(1, ny):
                    mid.append(near(2 + ny + d, flip(z, 2) * ny + lax.rem(y - d + ny, ny)))
            else:
                arrive(mid)
                over.extend(across(stage, 3, flip(z, 3), slot))

        def four():
            arrive([first] + ends[: ny - 1] + mid if flat else over)

        return [one, two, three, four]

    other = x * cores + 1 - core

    def twin(stage, k, source, target):
        return [toss(stage, nx + k, source, target, other)]

    def spread_start(stage, source, slot):
        along = [toss(stage, k, source, slot(c), lax.rem(x + k, nx) * cores + core) for k in range(1, nx)]
        return along, twin(stage, 0, source, slot(c))

    def spread_end(stage, state, slot):
        along, near = state
        for k in range(1, nx):
            along[k - 1].wait_recv()
            here = slot(lax.rem(x - k + nx, nx) * cores + core)
            near = near + twin(stage, k, here, here)
        return near

    def row_stage(stage, source, target):
        peers = [lax.rem(r + d, nr) for d in range(1, nr)]
        return [push(stage, d, source(p), target, p) for d, p in enumerate(peers, 1)]

    def fold_near(stage, block, got):
        return [toss(stage, q, block(q * cores + 1 - core), got.at[q], other) for q in range(nx)]

    def fold_far(stage, copies, block, near, send, got):
        arrive(copies)
        out = []
        for k in [*range(1, nx), 0]:
            q = lax.rem(x + k, nx)
            total = block(q * cores + core)[...] + near[q]
            if k:
                send[k] = total
                out.append(toss(stage, nx + k, send.at[k], got.at[k], q * cores + core))
            else:
                got[0] = total
        return out

    def fold_end(copies, got):
        arrive(copies)
        total = got[0]
        for k in range(1, nx):
            total = total + got[k]
        return total

    lslot = [lambda i: xl.at[0, i], lambda i: xl.at[1, i]]
    uslot = [lambda i: xu.at[0, i], lambda i: xu.at[1, i]]
    for copy in own:
        copy.wait()
    low = [spread_start(0, xl.at[0, c], lslot[0]), spread_start(1, xl.at[1, c], lslot[1])]
    up = [gather(0, xu.at[0, r], uslot[0], False), gather(1, xu.at[1, r], uslot[1], True)]
    for copy in loads:
        copy.wait()
    iuo, iun = split(sq[0]), split(sq[2])
    mix_u = split(mul(split(mul(iuo, split(sq[1]))), iun))
    ilo = sq[5]
    mix_l = mul(split(mul(split(sq[3]), split(sq[4]))), split(ilo))
    mix_l, ilo, iln = split(mix_l.T), split(ilo.T), split(sq[3].T)
    load.wait()
    high, rest = split(a_ref[...])
    ah[...] = high
    al[...] = rest
    q = {}
    b0, b1 = {}, {}
    each, few = width // nc, width // nc // nr
    part = lambda p: pt.at[pl.ds(pl.multiple_of(p * each, each), each)]
    piece = lambda p: ps.at[lrow(p)]
    half = lambda i: gp.at[:, pl.ds(pl.multiple_of(i * width, width), width)]
    cslot = lambda i: both_ref.at[core, urow(i)]

    def lower():
        near = spread_end(0, low[0], lslot[0])
        near = near + spread_end(1, low[1], lslot[1])
        arrive(near)
        ln, lo = split(xl[0].reshape(width, rows)), split(xl[1].reshape(width, rows))
        lts = split(mul(ilo, lo) - mul(mix_l, ln))
        q["lns"] = split(mul(iln, ln))
        for i in range(cols // width):
            here = slice(i * width, (i + 1) * width)
            pb[:, here] = -mul(lts, (ah[:, here], al[:, here]))

    def spill(k):
        zt = reach(k) if k else z
        peers = [zt * ny + lax.rem(y + d, ny) for d in range(1, ny)]
        b0[k] = [
            push(4, k * ny + d, pb.at[urow(p)], ry.at[k, d], z * ny + lax.rem(y + d, ny))
            for d, p in enumerate(peers, 1)
        ]

    def pile(k):
        arrive(b0[k])
        zt = reach(k) if k else z
        total = pb[urow(zt * ny + y)]
        for d in range(1, ny):
            total = total + ry[k, d]
        if k:
            sz[k] = total
            b1[k] = push(5, k, sz.at[k], rz.at[k], zt * ny + y)
        else:
            rz[0] = total

    def band():
        arrive([b1[k] for k in hops])
        total = rz[0]
        for k in hops:
            total = total + rz[k]
        bc[...] = total
        band_ref[urow(r)] = total
        q["b"] = gather(2, bc, lambda i: band_ref.at[urow(i)], False)

    def upper():
        for i in range(cols // width):
            here = slice(i * width, (i + 1) * width)
            un, uo = split(xu[0, :, :, here].reshape(width, width)), split(xu[1, :, :, here].reshape(width, width))
            vh[:width, here], vl[:width, here] = split(mul(iuo, uo) - mul(mix_u, un))
        for i in range(rows // width):
            here = slice(i * width, (i + 1) * width)
            ps[here] = -mul((ah[here], al[here]), (vh[:width], vl[:width]), NT)
        pt[...] = -mul(q["lns"], split(ps[...]))
        q["t0"] = fold_near(3, part, nt)
        for i in range(cols // width):
            here = slice(i * width, (i + 1) * width)
            un = split(xu[0, :, :, here].reshape(width, width))
            vh[width:, here], vl[width:, here] = split(mul(iun, un))

    def wide(stage, source, target):
        out = []
        for n in range(1, nx * nr):
            qx, p = lax.rem(x + n // nr, nx), lax.rem(r + n % nr, nr)
            peer = {"row": p, "col": qx * cores + core}
            out.append(put(None, peer, source(qx, p), target, ws_send.at[stage, n], ws_recv.at[stage, n]))
        return out

    def tell():
        for k in range(1, nx):
            peer = lax.rem(x + k, nx) * cores + core
            pl.semaphore_signal(ready, inc=1, device_id={"col": peer}, device_id_type=pl.DeviceIdType.MESH)

    def top_far():
        pl.semaphore_wait(ready, nx - 1)
        arrive(q["t0"])
        for i in range(nx):
            total = part(i * cores + core)[...] + nt[i]
            for k in range(nr):
                st[i, k] = total[k * few : (k + 1) * few]
        q["t1"] = wide(0, lambda i, p: st.at[i, p], tt.at[x, r])
        tt[x, r] = st[x, r]

    def inner():
        gp[...] = -mul(split(bc[...]), (vh[...], vl[...]), NT)
        q["g0"] = [toss(4, 0, half(1 - core), gn, other)]
        q["p0"] = fold_near(2, piece, fp)

    def inner_far():
        arrive(q["g0"])
        gr[0] = half(core)[...] + gn[...]
        q["g0"] = [toss(4, k, gr.at[0], gr.at[k], lax.rem(x + k, nx) * cores + core) for k in range(1, nx)]

    def strip_far():
        q["p0"] = fold_far(2, q["p0"], piece, fp, tp, rp)

    def inner_row():
        total = fold_end(q["g0"], gr)
        gc[...] = total
        both_ref[core, urow(r)] = total
        q["g"] = row_stage(3, lambda p: gc, cslot(r))

    def top_back():
        arrive(q["t1"])
        total = None
        for i in range(nx):
            for k in range(nr):
                total = tt[i, k] if total is None else total + tt[i, k]
        top_ref[c, r] = total
        q["t2"] = wide(1, lambda i, p: top_ref.at[c, r], top_ref.at[c, r])

    def top_twin():
        arrive(q["t2"])
        mine = [top_ref.at[i * cores + core] for i in range(nx)]
        q["t3"] = [toss(3, nx + i, ref, ref, other) for i, ref in enumerate(mine)]

    def strip_end():
        strip_ref[...] = fold_end(q["p0"], rp)

    def swap():
        arrive(q["g"])
        q["g2"] = toss(4, nx, both_ref.at[core], both_ref.at[core], other)

    far_first = hops[nz // 2 - 1 : nz // 2] + [k for k in hops[::-1] if k != nz // 2] + [0]
    up[0][0]()
    up[1][0]()
    up[0][1]()
    lower()
    for k in far_first:
        spill(k)
    up[1][1]()
    for k in far_first[:1]:
        pile(k)
    up[0][2]()
    for k in far_first[1:]:
        pile(k)
    up[1][2]()
    up[0][3]()
    up[1][3]()
    tell()
    band()
    upper()
    top_far()
    inner()
    inner_far()
    q["b"][0]()
    q["b"][1]()
    top_back()
    inner_row()
    strip_far()
    q["b"][2]()
    top_twin()
    swap()
    strip_end()
    q["b"][3]()
    arrive(q["t3"])
    arrive([q["g2"]])
    for copy in sent:
        copy.wait_send()


def finish(strip_ref, band_ref, both_ref, top_ref, corner, top, bottom, left, right, sem):
    pairs = (
        (band_ref, right), (strip_ref, bottom), (top_ref, top),
        (both_ref.at[0], corner), (both_ref.at[1], left),
    )
    copies = [pltpu.make_async_copy(source, target, sem.at[i]) for i, (source, target) in enumerate(pairs)]
    for copy in copies:
        copy.start()
    for copy in copies:
        copy.wait()


def body(an, ln, un, lot, lo, uol, uo, dln, dun, iln, iun, dlo, duo, ilo, iuo):
    nr, nc = lax.axis_size("row"), lax.axis_size("col")
    rows, cols = an.shape
    width = iln.shape[0]
    hu, wl, each = width // nr, rows // nc, width // nc
    ny = nc // 2 if nr % (nc // 2) == 0 else 1
    nz = nr // ny
    vm = pl.BlockSpec(memory_space=pltpu.VMEM)
    hbm = pl.BlockSpec(memory_space=pltpu.HBM)
    V, D = pltpu.VMEM, pltpu.SemaphoreType.DMA
    lanes = max(nr, 3 + (2 + nz) * ny)
    whole = V((nc // 2, nr, each // nr, width), f32)
    operands = (an, un, uo, ln.T, lo.T, lot, uol, iln, iun, ilo, iuo)
    strip, band, both, top = pl.pallas_call(
        functools.partial(kernel, nr, nc, ny),
        out_shape=(
            V((wl, width), f32), V((width, cols), f32), V((2, width, width), f32), V((nc, nr, each // nr, width), f32)
        ),
        in_specs=[hbm] * 11,
        out_specs=(vm, vm, vm, vm),
        scratch_shapes=[
            V((rows, cols), f32), V((rows, cols), bf16), V((rows, cols), bf16),
            V((2, nr, hu, cols), f32), V((2, nc, each, rows), f32),
            V((2 * width, cols), bf16), V((2 * width, cols), bf16),
            V((width, cols), f32), V((rows, width), f32),
            V((nz, ny, hu, cols), f32), V((nz, hu, cols), f32), V((nz, hu, cols), f32),
            *[V((nc // 2, wl, width), f32)] * 3, V((hu, cols), f32),
            V((hu, 2 * width), f32), V((hu, width), f32), V((nc // 2, hu, width), f32), V((hu, width), f32),
            V((width, width), f32), V((nc // 2, each, width), f32), whole, whole,
            V((6, width, width), f32),
            D, D((6,)), D((4,)), D((6, lanes)), D((6, lanes)), D((6, nc)), D((6, nc)), D((2, nc // 2 * nr)), D((2, nc // 2 * nr)), pltpu.SemaphoreType.REGULAR,
        ],
        compiler_params=pltpu.CompilerParams(collective_id=0, has_side_effects=True, vmem_limit_bytes=LIMIT),
    )(*[pltpu.with_memory_space_constraint(v, pltpu.HBM) for v in operands])
    shapes = [(width, width), (width, width), strip.shape, (width, width), band.shape]
    return pl.pallas_call(
        finish,
        out_shape=[jax.ShapeDtypeStruct(shape, f32) for shape in shapes],
        in_specs=[vm] * 4,
        out_specs=[hbm] * 5,
        scratch_shapes=[D((5,))],
        compiler_params=pltpu.CompilerParams(vmem_limit_bytes=1 << 20),
    )(strip, band, both, top.reshape(width, width))


def solution(mesh):
    two, whole = P("row", "col"), P()
    return jax.shard_map(
        body,
        mesh=mesh,
        in_specs=(two, two, two, whole, two, whole, two) + (whole,) * 8,
        out_specs=(P(), P(), P(("row", "col"), None), P(), P(None, "col")),
        check_vma=False,
    )
```
